512 devices in a mesh: row: 32 (over y_hi, z), col: 16 (over x, y_lo, core).
Axes of the slice: x: 4, y: 8 (y_hi: 4, y_lo: 2; y = y_hi * 2 + y_lo), z: 8, core: 2. Of those that a mesh axis runs over, the one named last changes fastest.
Arguments:
- anc_inverse: bfloat16 [1, 32, 256, 2, 16, 256], P(None, 'row', None, None, 'col'), may hold values from -6 to 6
- factor_one: bfloat16 [1, 32, 256, 2, 16, 256], P(None, 'row', None, None, 'col'), may hold values from -0.0625 to 0.0625
- factor_two: bfloat16 [1, 32, 256, 1, 16, 256], P(None, 'row', None, None, 'col'), may hold values from -0.0625 to 0.0625
- parent_block: bfloat16 [1, 16, 256, 256], P(None, 'col'), may hold values from -0.375 to 0.375
- diag_one: float32 [2, 16, 256, 256], P(None, 'col'), may hold values from -6 to 6
- diag_two: float32 [1, 16, 256, 256], P(None, 'col'), may hold values from -6 to 6
- pattern_one: int32 [1, 32, 2, 16], P(None, 'row', None, 'col'), may hold values from 0 to 1
- pattern_two: int32 [1, 32, 1, 16], P(None, 'row', None, 'col'), may hold values from 0 to 1, as said below
- parent: int32 [1, 16], P(None, 'col'), may hold values from 0 to 31, as said below
Outputs:
- inv_one: bfloat16 [1, 32, 256, 2, 16, 256], P(None, 'row', None, None, 'col')
- diag_inv_one: float32 [2, 16, 256, 256], P(None, 'col')
- inv_two: bfloat16 [1, 32, 256, 1, 16, 256], P(None, 'row', None, None, 'col')
- parent_inv: bfloat16 [1, 16, 256, 256], P(None, 'col')
- diag_inv_two: float32 [1, 16, 256, 256], P(None, 'col')
The draws below stay inside these ranges and needn't reach their ends.
Inputs may be any that keep to these rules, and one draw needn't show every extreme that they name: pattern_two[J, K] is zero wherever pattern_one[J, P(K)] is zero. parent[k, c] is a level-one supernode whose index leaves remainder c when divided by 16.
All inputs are finite; a program needn't handle non-finite values.
Results may differ from the reference program's by a relative error of at most 0.007.
Values may be sent and summed in bfloat16 or wider, within the bound.
A program may use at most 64 MiB of HBM per device.

```python
import jax
import jax.numpy as jnp
from jax import lax

B = 256
AR = 1
PC = 2
CC = 1
NA = 32
NP = 32
NC = 16
N_ROW = 32
N_COL = 16


def tree_draws(key):
    first_mask = jax.random.randint(jax.random.fold_in(key, 101), (AR, N_ROW, PC, N_COL), 0, 2).astype(jnp.int32)
    local_parent = jax.random.randint(jax.random.fold_in(key, 102), (CC, N_COL), 0, PC).astype(jnp.int32)
    local_parent = local_parent.at[0, 0].set(0).at[0, N_COL - 1].set(PC - 1)
    column_ids = jnp.arange(N_COL, dtype=jnp.int32)[None, :]
    parent_ids = local_parent * N_COL + column_ids
    keep_mask = (jax.random.randint(jax.random.fold_in(key, 103), (AR, N_ROW, CC, N_COL), 0, 4) > 0).astype(jnp.int32)
    spread = jnp.broadcast_to(local_parent[None, None], (AR, N_ROW, CC, N_COL))
    above_mask = jnp.take_along_axis(first_mask, spread, axis=2)
    return (first_mask, above_mask * keep_mask, parent_ids)


def draw_pattern_one(key, part):
    return tree_draws(key)[0]


def draw_pattern_two(key, part):
    return tree_draws(key)[1]


def draw_parent(key, part):
    return tree_draws(key)[2]


def shard_levels(stream_key, dims, split, smallest, high):
    factor_of = 1.0
    for position, blocks in split:
        draws = jax.random.uniform(jax.random.fold_in(jax.random.fold_in(stream_key, 6), position), (blocks,), jnp.float32, smallest / len(split), high / len(split))
        factor_of = factor_of * jnp.repeat(jnp.exp(draws), dims[position] // blocks).reshape((-1,) + (1,) * (len(dims) - 1 - position))
    return factor_of


def centred(stream_key, extent, scale, reach, split=(), kind=jnp.bfloat16):
    entries = scale * jax.random.normal(stream_key, extent, jnp.float32)
    if split:
        entries = entries * shard_levels(stream_key, extent, split, -0.22, 0.18)
    return jnp.clip(entries, -reach, reach).astype(kind)


def setup_inputs(seed: int = 0) -> dict:
    splits = jax.random.split(jax.random.key(seed), 10)
    return {
        "anc_inverse": centred(splits[0], (AR, N_ROW, B, NA // N_COL, N_COL, B), 1.0, 6.0, ((1, 32), (4, 16))),
        "factor_one": centred(splits[1], (AR, N_ROW, B, PC, N_COL, B), (NA * B) ** -0.5, 0.0625, ((1, 32), (4, 16))),
        "factor_two": centred(splits[2], (AR, N_ROW, B, CC, N_COL, B), (NA * B) ** -0.5, 0.0625, ((1, 32), (4, 16))),
        "parent_block": centred(splits[3], (CC, N_COL, B, B), B ** -0.5, 0.375, ((1, 16),)),
        "diag_one": centred(splits[4], (PC, N_COL, B, B), 1.0, 6.0, ((1, 16),), jnp.float32),
        "diag_two": centred(splits[5], (CC, N_COL, B, B), 1.0, 6.0, ((1, 16),), jnp.float32),
        "pattern_one": draw_pattern_one(jax.random.fold_in(splits[9], 71), 0),
        "pattern_two": draw_pattern_two(jax.random.fold_in(splits[9], 71), 0),
        "parent": draw_parent(jax.random.fold_in(splits[9], 71), 0),
    }


def rounded(value):
    return lax.optimization_barrier(value.astype(jnp.bfloat16)).astype(jnp.float32)


def reference(anc_inverse, factor_one, factor_two, parent_block, diag_one, diag_two, pattern_one, pattern_two, parent):
    ancestors = anc_inverse.reshape(NA * B, NA * B)
    first_mask = pattern_one.reshape(NA, 1, NP, 1)
    first_factor = factor_one.reshape(NA, B, NP, B) * first_mask.astype(jnp.bfloat16)
    first_total = jnp.dot(ancestors, first_factor.reshape(NA * B, NP * B), preferred_element_type=jnp.float32)
    first_inv = (-first_total.reshape(NA, B, NP, B) * first_mask.astype(jnp.float32)).astype(jnp.bfloat16)
    first_wide = first_factor.astype(jnp.float32)
    inv_wide = first_inv.astype(jnp.float32)
    first_diag = diag_one.reshape(NP, B, B) - jnp.einsum("ixky,ixkz->kyz", first_wide, inv_wide)
    parent_ids = parent.reshape(NC).astype(jnp.int32)
    second_mask = pattern_two.reshape(NA, 1, NC, 1)
    second_factor = factor_two.reshape(NA, B, NC, B) * second_mask.astype(jnp.bfloat16)
    second_wide = second_factor.astype(jnp.float32)
    parent_cols = jnp.take(inv_wide, parent_ids, axis=2)
    cross = jnp.einsum("ixky,ixkz->kyz", parent_cols, second_wide)
    coupling = parent_block.reshape(NC, B, B).astype(jnp.float32)
    parent_diag = rounded(jnp.take(first_diag, parent_ids, axis=0))
    parent_inv = (-(jnp.einsum("kyx,kxz->kyz", parent_diag, coupling) + cross)).astype(jnp.bfloat16)
    second_total = jnp.dot(ancestors, second_factor.reshape(NA * B, NC * B), preferred_element_type=jnp.float32)
    side = jnp.einsum("ixky,kyz->ixkz", parent_cols, coupling)
    second_inv = (-(second_total.reshape(NA, B, NC, B) + side) * second_mask.astype(jnp.float32)).astype(jnp.bfloat16)
    child_terms = jnp.einsum("ixky,ixkz->kyz", second_wide, second_inv.astype(jnp.float32))
    parent_terms = jnp.einsum("kxy,kxz->kyz", coupling, parent_inv.astype(jnp.float32))
    second_diag = diag_two.reshape(NC, B, B) - (child_terms + parent_terms)
    return (first_inv.reshape(AR, N_ROW, B, PC, N_COL, B), first_diag.reshape(PC, N_COL, B, B), second_inv.reshape(AR, N_ROW, B, CC, N_COL, B), parent_inv.reshape(CC, N_COL, B, B), second_diag.reshape(CC, N_COL, B, B))
```

```python
import functools

import jax
import jax.numpy as jnp
from jax import lax
from jax.experimental import pallas as pl
from jax.experimental.pallas import tpu as pltpu
from jax.sharding import PartitionSpec as P

MESH = pl.DeviceIdType.MESH
B = 256
NY, NZ, NX = 4, 8, 4
ROWS = NY * NZ
WIDE = 3 * B
SLICE = 4 * B // ROWS


def mm(a, b):
    return jnp.dot(a, b, preferred_element_type=jnp.float32)


def mm_t(a, b):
    return lax.dot_general(a, b, (((0,), (0,)), ((), ())), preferred_element_type=jnp.float32)


def kernel(
    p1_ref, p2_ref, par_ref, a_ref, f_ref, pb_ref, d1_ref, d2_ref,
    inv1_ref, diag1_ref, inv2_ref, pinv_ref, diag2_ref,
    f_all, a_all, acc, c_send, c_recv, parts, r_recv, r_out,
    fs, fr, a1s, a1r, xs, xr, ys, yr, cs, cr, rs, rr, s1, r1, s2, r2, own_sem,
):
    row, col = lax.axis_index("row"), lax.axis_index("col")
    y, z = row // NZ, row % NZ
    x, yl, core = col // 4, (col // 2) % 2, col % 2

    def remote(src, dst, ss, rs_, to_row, to_col):
        return pltpu.make_async_remote_copy(
            src_ref=src, dst_ref=dst, send_sem=ss, recv_sem=rs_,
            device_id=(to_row, to_col), device_id_type=MESH,
        )

    def row_at(d):
        return lax.rem(row + d, ROWS)

    def col_of(x_, yl_, core_):
        return x_ * 4 + yl_ * 2 + core_

    y_mate = col_of(x, 1 - yl, core)
    c_mate = col_of(x, yl, 1 - core)

    barrier = pltpu.get_barrier_semaphore()

    def greet(d, carry):
        pl.semaphore_signal(barrier, inc=1, device_id=(row_at(d), col), device_id_type=MESH)
        return carry

    lax.fori_loop(1, ROWS, greet, 0)
    for dx in range(1, NX):
        pl.semaphore_signal(
            barrier, inc=1, device_id=(row, col_of(lax.rem(x + dx, NX), yl, core)), device_id_type=MESH
        )
    pl.semaphore_signal(barrier, inc=1, device_id=(row, y_mate), device_id_type=MESH)
    pl.semaphore_signal(barrier, inc=1, device_id=(row, c_mate), device_id_type=MESH)
    pl.semaphore_wait(barrier, ROWS - 1 + NX - 1 + 2)

    up = y * NZ + lax.rem(z + 1, NZ)
    down = y * NZ + lax.rem(z + NZ - 1, NZ)
    half = B // 2

    def f_copies(step):
        up_slot = lax.rem(z + NZ - step, NZ)
        down_slot = lax.rem(z + step, NZ)
        if step == 0:
            u_src, d_src = f_ref, f_ref
        elif step < 3:
            u_src, d_src = f_all.at[up_slot], f_all.at[down_slot]
        if step < 3:
            u_dst, d_dst = f_all.at[up_slot], f_all.at[down_slot]
        else:
            u_src = u_dst = f_all.at[up_slot, pl.ds(0, half)]
            d_src = d_dst = f_all.at[down_slot, pl.ds(half, half)]
        return (
            remote(u_src, u_dst, fs.at[0, step], fr.at[0, step], up, col),
            remote(d_src, d_dst, fs.at[1, step], fr.at[1, step], down, col),
        )

    def f_start(step):
        for copy in f_copies(step):
            copy.start()

    def f_arrived(step):
        for copy in f_copies(step):
            copy.wait_recv()

    slot = lax.rem(col, NZ)
    holder = lax.rem(y, 2) == x // 2

    def a1_copy(h):
        return remote(
            a_ref.at[h], a_all.at[slot, y], a1s.at[h], a1r.at[y], (2 * h + x // 2) * NZ + z, col
        )

    def own_copy(h):
        return pltpu.make_async_copy(a_ref.at[h], a_all.at[slot, y], own_sem)

    f_start(0)
    for h in range(2):
        target = 2 * h + x // 2

        @pl.when(target != y)
        def _():
            a1_copy(h).start()

        @pl.when(target == y)
        def _():
            own_copy(h).start()

    def slot_of(s, yl_, core_):
        return s * 4 + yl_ * 2 + core_

    def x_copy(s, dx):
        k = slot_of(s, yl, core)
        return remote(
            a_all.at[k], a_all.at[k], xs.at[dx - 1], xr.at[s], row, col_of(lax.rem(x + dx, NX), yl, core)
        )

    def y_copy(s):
        k = slot_of(s, yl, core)
        return remote(a_all.at[k], a_all.at[k], ys.at[s], yr.at[s], row, y_mate)

    def y_here(s):
        k = slot_of(s, 1 - yl, core)
        return remote(a_all.at[k], a_all.at[k], ys.at[s], yr.at[s], row, y_mate)

    def c_copy(s, yl_):
        k = slot_of(s, yl_, core)
        return remote(a_all.at[k], a_all.at[k], cs.at[s, yl_], cr.at[s, yl_], row, c_mate)

    def c_here(s, yl_):
        k = slot_of(s, yl_, 1 - core)
        return remote(a_all.at[k], a_all.at[k], cs.at[s, yl_], cr.at[s, yl_], row, c_mate)

    f_all[z] = f_ref[...]
    f_arrived(0)
    f_start(1)

    @pl.when(holder)
    def _():
        own_copy(0).wait()
        for k in range(1, NY):
            other = lax.rem(y + k, NY)
            remote(
                a_ref.at[0], a_all.at[slot, other], a1s.at[0], a1r.at[other], row_at(1), col
            ).wait_recv()
        s = lax.rem(x, 2)
        for dx in (2, 1, 3):
            x_copy(s, dx).start()

    f_arrived(1)
    f_start(2)
    for s in range(2):
        source = 2 * lax.rem(y, 2) + s

        @pl.when(source != x)
        def _():
            x_copy(s, 1).wait_recv()

        y_copy(s).start()
        c_copy(s, yl).start()
    f_arrived(2)
    f_start(3)
    for s in range(2):
        y_here(s).wait_recv()
        c_copy(s, 1 - yl).start()
    f_arrived(3)
    for s in range(2):
        for yl_ in range(2):
            c_here(s, yl_).wait_recv()

    def partial_product(y_):
        acc[...] = mm(a_all[0, y_], f_all[0])

        def step(k, carry):
            acc[...] += mm(a_all[k, y_], f_all[k])
            return carry

        lax.fori_loop(1, NZ, step, 0)

    def c_part(k):
        return remote(
            c_send.at[k - 1], c_recv.at[k - 1], rs.at[k - 1], rr.at[k - 1], lax.rem(y + k, NY) * NZ + z, col
        )

    for k in (2, 1, 3):
        partial_product(lax.rem(y + k, NY))
        c_send[k - 1] = acc[...].astype(jnp.bfloat16)
        c_part(k).start()
    partial_product(y)
    for k in (1, 3, 2):
        c_part(k).wait_recv()
    total = acc[...]
    for k in (1, 2, 3):
        total += c_recv[k - 1].astype(jnp.float32)

    m0 = p1_ref[0].astype(jnp.float32)
    m1 = p1_ref[1].astype(jnp.float32)
    m2 = p2_ref[0].astype(jnp.float32)
    second = par_ref[0] >= 16
    inv_a = (-total[:, :B] * m0).astype(jnp.bfloat16)
    inv_b = (-total[:, B : 2 * B] * m1).astype(jnp.bfloat16)
    parent_cols = jnp.where(second, inv_b, inv_a)
    pb = pb_ref[...]
    side = mm(parent_cols, pb)
    inv_c = (-(total[:, 2 * B :] + side) * m2).astype(jnp.bfloat16)
    inv1_ref[0] = inv_a
    inv1_ref[1] = inv_b
    inv2_ref[...] = inv_c
    per = B // SLICE

    def put(i, value):
        parts[pl.ds(i * per, per)] = value.astype(jnp.bfloat16).reshape(per, SLICE, B)

    put(0, mm_t(f_ref[:, :B], inv_a))
    put(1, mm_t(f_ref[:, B : 2 * B], inv_b))
    put(2, mm_t(parent_cols, f_ref[:, 2 * B :]))
    put(3, mm_t(f_ref[:, 2 * B :], inv_c))

    def first(d):
        return remote(parts.at[row_at(d)], r_recv.at[d], s1.at[d], r1.at[d], row_at(d), col)

    def second_copy(d):
        return remote(r_out.at[row], r_out.at[row], s2.at[d], r2.at[d], row_at(d), col)

    def loop(body):
        def step(d, carry):
            body(d)
            return carry

        lax.fori_loop(1, ROWS, step, 0)

    loop(lambda d: first(d).start())
    r_recv[0] = parts[row]
    loop(lambda d: first(d).wait_recv())
    r_out[row] = jnp.sum(r_recv[...].astype(jnp.float32), axis=0).astype(jnp.bfloat16)
    loop(lambda d: second_copy(d).start())
    loop(lambda d: second_copy(d).wait_recv())

    def block(i):
        return r_out[pl.ds(i * per, per)].reshape(B, B).astype(jnp.float32)

    diag_a = d1_ref[0] - block(0)
    diag_b = d1_ref[1] - block(1)
    diag1_ref[0] = diag_a
    diag1_ref[1] = diag_b
    parent_diag = jnp.where(second, diag_b, diag_a).astype(jnp.bfloat16)
    pinv = (-(mm(parent_diag, pb) + block(2))).astype(jnp.bfloat16)
    pinv_ref[...] = pinv
    diag2_ref[...] = d2_ref[...] - (block(3) + mm_t(pb, pinv))

    for step in range(4):
        for copy in f_copies(step):
            copy.wait_send()
    for h in range(2):

        @pl.when(2 * h + x // 2 != y)
        def _():
            a1_copy(h).wait_send()

    @pl.when(holder)
    def _():
        for dx in range(1, NX):
            x_copy(0, dx).wait_send()

    for s in range(2):
        y_copy(s).wait_send()
        for yl_ in range(2):
            c_copy(s, yl_).wait_send()
    for k in range(1, NY):
        c_part(k).wait_send()
    loop(lambda d: first(d).wait_send())
    loop(lambda d: second_copy(d).wait_send())


def body(anc, one, two, pb, d1, d2, p1, p2, par):
    a = anc.reshape(B, 2, B).transpose(1, 0, 2)
    f1 = one.reshape(B, 2, B) * p1.reshape(1, 2, 1).astype(jnp.bfloat16)
    f2 = two.reshape(B, 1, B) * p2.reshape(1, 1, 1).astype(jnp.bfloat16)
    f = jnp.concatenate([f1, f2], axis=1).reshape(B, WIDE)
    vmem = pl.BlockSpec(memory_space=pltpu.VMEM)
    smem = pl.BlockSpec(memory_space=pltpu.SMEM)
    dma = pltpu.SemaphoreType.DMA
    bf, f32 = jnp.bfloat16, jnp.float32
    inv1, diag1, inv2, pinv, diag2 = pl.pallas_call(
        kernel,
        out_shape=(
            jax.ShapeDtypeStruct((2, B, B), bf),
            jax.ShapeDtypeStruct((2, B, B), f32),
            jax.ShapeDtypeStruct((B, B), bf),
            jax.ShapeDtypeStruct((B, B), bf),
            jax.ShapeDtypeStruct((B, B), f32),
        ),
        in_specs=[smem] * 3 + [vmem] * 5,
        out_specs=(vmem,) * 5,
        scratch_shapes=[
            pltpu.VMEM((NZ, B, WIDE), bf),
            pltpu.VMEM((NZ, NY, B, B), bf),
            pltpu.VMEM((B, WIDE), f32),
            pltpu.VMEM((3, B, WIDE), bf),
            pltpu.VMEM((3, B, WIDE), bf),
            pltpu.VMEM((ROWS, SLICE, B), bf),
            pltpu.VMEM((ROWS, SLICE, B), bf),
            pltpu.VMEM((ROWS, SLICE, B), bf),
            dma((2, 4)), dma((2, 4)),
            dma((2,)), dma((NY,)),
            dma((3,)), dma((2,)),
            dma((2,)), dma((2,)),
            dma((2, 2)), dma((2, 2)),
            dma((3,)), dma((3,)),
            dma((ROWS,)), dma((ROWS,)),
            dma((ROWS,)), dma((ROWS,)),
            dma(()),
        ],
        compiler_params=pltpu.CompilerParams(
            collective_id=0, has_side_effects=True, vmem_limit_bytes=40 * 1024 * 1024
        ),
    )(
        p1.reshape(2), p2.reshape(1), par.reshape(1), a, f,
        pb.reshape(B, B), d1.reshape(2, B, B), d2.reshape(B, B),
    )
    return (
        inv1.transpose(1, 0, 2).reshape(one.shape),
        diag1.reshape(d1.shape),
        inv2.reshape(two.shape),
        pinv.reshape(pb.shape),
        diag2.reshape(d2.shape),
    )


def solution(mesh):
    placed = (
        P(None, "row", None, None, "col", None),
        P(None, "row", None, None, "col", None),
        P(None, "row", None, None, "col", None),
        P(None, "col", None, None),
        P(None, "col", None, None),
        P(None, "col", None, None),
        P(None, "row", None, "col"),
        P(None, "row", None, "col"),
        P(None, "col"),
    )
    return jax.shard_map(
        body,
        mesh=mesh,
        in_specs=placed,
        out_specs=(
            P(None, "row", None, None, "col", None),
            P(None, "col", None, None),
            P(None, "row", None, None, "col", None),
            P(None, "col", None, None),
            P(None, "col", None, None),
        ),
        check_vma=False,
    )
```

```python
import functools

import jax
import jax.numpy as jnp
from jax import lax
from jax.experimental import pallas as pl
from jax.experimental.pallas import tpu as pltpu
from jax.sharding import PartitionSpec as P

MESH = pl.DeviceIdType.MESH
B = 256
NY, NZ, NX = 4, 8, 4
ROWS = NY * NZ
SLICE = 4 * B // ROWS


def mm(a, b):
    return jnp.dot(a, b, preferred_element_type=jnp.float32)


def mm_t(a, b):
    return lax.dot_general(a, b, (((0,), (0,)), ((), ())), preferred_element_type=jnp.float32)


def kernel(
    p1_ref, p2_ref, par_ref, a_ref, f1_ref, f2_ref, pb_ref, d1_ref, d2_ref,
    inv1_ref, diag1_ref, inv2_ref, pinv_ref, diag2_ref,
    f_all, a_all, acc, e_send, e_recv, p_send, p_recv, g_send, g_recv, parts, r_recv, r_out,
    fs, fr, a1s, a1r, os, orr, xs, xr, ys, yr, cs, cr, es, er, ps, pr, gs, gr, s1, r1, s2, r2, own_sem,
):
    row, col = lax.axis_index("row"), lax.axis_index("col")
    y, z = row // NZ, row % NZ
    x, yl, core = col // 4, (col // 2) % 2, col % 2

    def remote(src, dst, ss, rs_, to_row, to_col):
        return pltpu.make_async_remote_copy(
            src_ref=src, dst_ref=dst, send_sem=ss, recv_sem=rs_,
            device_id=(to_row, to_col), device_id_type=MESH,
        )

    def row_at(d):
        return lax.rem(row + d, ROWS)

    def col_of(x_, yl_, core_):
        return x_ * 4 + yl_ * 2 + core_

    y_mate = col_of(x, 1 - yl, core)
    c_mate = col_of(x, yl, 1 - core)
    across = col_of(x + 1 - 2 * lax.rem(x, 2), yl, core)
    outward = col_of(NX - 1 - x, yl, core)

    barrier = pltpu.get_barrier_semaphore()

    def greet(d, carry):
        pl.semaphore_signal(barrier, inc=1, device_id=(row_at(d), col), device_id_type=MESH)
        return carry

    lax.fori_loop(1, ROWS, greet, 0)
    for mate in (across, outward, y_mate, c_mate):
        pl.semaphore_signal(barrier, inc=1, device_id=(row, mate), device_id_type=MESH)
    m0 = p1_ref[0].astype(jnp.float32)
    m1 = p1_ref[1].astype(jnp.float32)
    m2 = p2_ref[0].astype(jnp.float32)
    f_all[0, z] = f1_ref[0] * m0.astype(jnp.bfloat16)
    f_all[1, z] = f1_ref[1] * m1.astype(jnp.bfloat16)
    f_all[2, z] = f2_ref[...] * m2.astype(jnp.bfloat16)
    pl.semaphore_wait(barrier, ROWS - 1 + 4)

    up = y * NZ + lax.rem(z + 1, NZ)
    down = y * NZ + lax.rem(z + NZ - 1, NZ)
    half = B // 2

    def f_copies(step, k):
        up_slot = lax.rem(z + NZ - step, NZ)
        down_slot = lax.rem(z + step, NZ)
        if step < 3:
            u, d = f_all.at[k, up_slot], f_all.at[k, down_slot]
        else:
            u = f_all.at[k, up_slot, pl.ds(0, half)]
            d = f_all.at[k, down_slot, pl.ds(half, half)]
        return (
            remote(u, u, fs.at[0, step, k], fr.at[0, step, k], up, col),
            remote(d, d, fs.at[1, step, k], fr.at[1, step, k], down, col),
        )

    def f_step(step):
        for k in range(3):
            if step > 0:
                for copy in f_copies(step - 1, k):
                    copy.wait_recv()
            if step < 4:
                for copy in f_copies(step, k):
                    copy.start()

    slot = lax.rem(col, NZ)
    hold = lax.rem(y + x // 2 + 1, 2)
    near = lax.rem(x + 1 + hold, 2)

    def a1_copy(h):
        return remote(
            a_ref.at[h], a_all.at[slot, y], a1s.at[h], a1r.at[y], (2 * h + x // 2) * NZ + z, col
        )

    def own_copy(h):
        return pltpu.make_async_copy(a_ref.at[h], a_all.at[slot, y], own_sem)

    for h in range(2):
        target = 2 * h + x // 2

        @pl.when(target != y)
        def _():
            a1_copy(h).start()

        @pl.when(target == y)
        def _():
            own_copy(h).start()

    f_step(0)

    def chunk(far, yl_, core_, k):
        s = 1 - near if far else near
        return a_all.at[s * 4 + yl_ * 2 + core_, lax.rem(y + k, NY)]

    def o_copy(k):
        c = chunk(0, yl, core, k)
        return remote(c, c, os.at[k], orr.at[k], row, outward)

    def x_copy(k, far=0):
        c = chunk(far, yl, core, k)
        return remote(c, c, xs.at[k], xr.at[k], row, across)

    def y_copy(far, k, yl_):
        c = chunk(far, yl_, core, k)
        return remote(c, c, ys.at[far, k], yr.at[far, k], row, y_mate)

    def c_copy(far, other, k, core_):
        c = chunk(far, 1 - yl if other else yl, core_, k)
        return remote(c, c, cs.at[far, other, k], cr.at[far, other, k], row, c_mate)

    def stage_a(k):
        @pl.when(hold == 1)
        def _():
            if k == 0:
                own_copy(0).wait()
            else:
                other = lax.rem(y + k, NY)
                remote(
                    a_ref.at[0], a_all.at[slot, other], a1s.at[0], a1r.at[other], row_at(1), col
                ).wait_recv()
            o_copy(k).start()

        @pl.when(hold == 0)
        def _():
            o_copy(k).wait_recv()

        x_copy(k).start()
        y_copy(0, k, yl).start()
        c_copy(0, 0, k, core).start()

    def stage_b(k):
        x_copy(k, 1).wait_recv()
        y_copy(1, k, yl).start()
        c_copy(1, 0, k, core).start()

    def stage_c(k):
        for far in range(2):
            y_copy(far, k, 1 - yl).wait_recv()
            c_copy(far, 1, k, core).start()

    stage_a(0)
    stage_a(1)
    f_step(1)
    stage_b(0)
    stage_a(3)
    stage_c(0)
    stage_b(1)
    stage_a(2)
    f_step(2)
    stage_c(1)
    stage_b(3)
    stage_b(2)
    f_step(3)
    stage_c(3)
    stage_c(2)
    f_step(4)
    for k in (0, 1, 3, 2):
        for other in range(2):
            for far in range(2):
                c_copy(far, other, k, 1 - core).wait_recv()

    y_up = lax.rem(y + 1, NY)
    y_down = lax.rem(y + NY - 1, NY)
    row_up, row_down = y_up * NZ + z, y_down * NZ + z

    def product(y_, k):
        left = jnp.concatenate([a_all[i, y_] for i in range(NZ)], axis=1)
        return mm(left, f_all[k].reshape(NZ * B, B))

    def pair(send, recv, ss, rs_, k):
        return (
            remote(send.at[k, 0], recv.at[k, 0], ss.at[k, 0], rs_.at[k, 0], row_up, col),
            remote(send.at[k, 1], recv.at[k, 1], ss.at[k, 1], rs_.at[k, 1], row_down, col),
        )

    def early(k):
        return pair(e_send, e_recv, es, er, k)

    def plain(k):
        return pair(p_send, p_recv, ps, pr, k)

    def grown(k):
        return pair(g_send, g_recv, gs, gr, k)

    bf = jnp.bfloat16
    for k in range(3):
        part = product(lax.rem(y + 2, NY), k).astype(bf)
        e_send[k, 0] = part[:half]
        e_send[k, 1] = part[half:]
        for copy in early(k):
            copy.start()
    for k in range(3):
        part = product(y_up, k)
        acc[0, k] = part[:half]
        p_send[k, 0] = part[half:].astype(bf)
        plain(k)[0].start()
        part = product(y_down, k)
        acc[1, k] = part[half:]
        p_send[k, 1] = part[:half].astype(bf)
        plain(k)[1].start()
    for k in range(3):
        for way in range(2):
            early(k)[way].wait_recv()
            g_send[k, way] = (acc[way, k] + e_recv[k, way].astype(jnp.float32)).astype(bf)
            grown(k)[way].start()
    for k in range(3):
        part = product(y, k)
        acc[2, k] = part[:half]
        acc[3, k] = part[half:]
    totals = []
    for k in range(3):
        for way in range(2):
            plain(k)[way].wait_recv()
            grown(k)[way].wait_recv()
        top = acc[2, k] + (g_recv[k, 0].astype(jnp.float32) + p_recv[k, 1].astype(jnp.float32))
        low_part = acc[3, k] + (p_recv[k, 0].astype(jnp.float32) + g_recv[k, 1].astype(jnp.float32))
        totals.append(jnp.concatenate([top, low_part], axis=0))

    second = par_ref[0] >= 16
    inv_a = (-totals[0] * m0).astype(bf)
    inv_b = (-totals[1] * m1).astype(bf)
    parent_cols = jnp.where(second, inv_b, inv_a)
    pb = pb_ref[...]
    side = mm(parent_cols, pb)
    inv_c = (-(totals[2] + side) * m2).astype(bf)
    inv1_ref[0] = inv_a
    inv1_ref[1] = inv_b
    inv2_ref[...] = inv_c
    per = B // SLICE

    def put(i, value):
        parts[pl.ds(i * per, per)] = value.astype(bf).reshape(per, SLICE, B)

    put(0, mm_t(f_all[0, z], inv_a))
    put(1, mm_t(f_all[1, z], inv_b))
    put(2, mm_t(parent_cols, f_all[2, z]))
    put(3, mm_t(f_all[2, z], inv_c))

    def first(d):
        return remote(parts.at[row_at(d)], r_recv.at[d], s1.at[d], r1.at[d], row_at(d), col)

    def second_copy(d):
        return remote(r_out.at[row], r_out.at[row], s2.at[d], r2.at[d], row_at(d), col)

    def loop(body):
        def step(d, carry):
            body(d)
            return carry

        lax.fori_loop(1, ROWS, step, 0)

    loop(lambda d: first(d).start())
    r_recv[0] = parts[row]
    loop(lambda d: first(d).wait_recv())
    r_out[row] = jnp.sum(r_recv[...].astype(jnp.float32), axis=0).astype(jnp.bfloat16)
    loop(lambda d: second_copy(d).start())
    loop(lambda d: second_copy(d).wait_recv())

    def block(i):
        return r_out[pl.ds(i * per, per)].reshape(B, B).astype(jnp.float32)

    diag_a = d1_ref[0] - block(0)
    diag_b = d1_ref[1] - block(1)
    diag1_ref[0] = diag_a
    diag1_ref[1] = diag_b
    parent_diag = jnp.where(second, diag_b, diag_a).astype(jnp.bfloat16)
    pinv = (-(mm(parent_diag, pb) + block(2))).astype(jnp.bfloat16)
    pinv_ref[...] = pinv
    diag2_ref[...] = d2_ref[...] - (block(3) + mm_t(pb, pinv))

    for k in range(3):
        for step in range(4):
            for copy in f_copies(step, k):
                copy.wait_send()
        for copies in (early(k), plain(k), grown(k)):
            for copy in copies:
                copy.wait_send()
    for h in range(2):

        @pl.when(2 * h + x // 2 != y)
        def _():
            a1_copy(h).wait_send()

    @pl.when(hold == 1)
    def _():
        for k in range(NY):
            o_copy(k).wait_send()

    for k in range(NY):
        x_copy(k).wait_send()
        for far in range(2):
            y_copy(far, k, yl).wait_send()
            for other in range(2):
                c_copy(far, other, k, core).wait_send()
    loop(lambda d: first(d).wait_send())
    loop(lambda d: second_copy(d).wait_send())


def body(anc, one, two, pb, d1, d2, p1, p2, par):
    a = anc.reshape(B, 2, B).transpose(1, 0, 2)
    f1 = one.reshape(B, 2, B).transpose(1, 0, 2)
    vmem = pl.BlockSpec(memory_space=pltpu.VMEM)
    smem = pl.BlockSpec(memory_space=pltpu.SMEM)
    dma = pltpu.SemaphoreType.DMA
    bf, f32 = jnp.bfloat16, jnp.float32
    inv1, diag1, inv2, pinv, diag2 = pl.pallas_call(
        kernel,
        out_shape=(
            jax.ShapeDtypeStruct((2, B, B), bf),
            jax.ShapeDtypeStruct((2, B, B), f32),
            jax.ShapeDtypeStruct((B, B), bf),
            jax.ShapeDtypeStruct((B, B), bf),
            jax.ShapeDtypeStruct((B, B), f32),
        ),
        in_specs=[smem] * 3 + [vmem] * 6,
        out_specs=(vmem,) * 5,
        scratch_shapes=[
            pltpu.VMEM((3, NZ, B, B), bf),
            pltpu.VMEM((NZ, NY, B, B), bf),
            pltpu.VMEM((4, 3, B // 2, B), f32),
        ]
        + [pltpu.VMEM((3, 2, B // 2, B), bf)] * 6
        + [pltpu.VMEM((ROWS, SLICE, B), bf)] * 3
        + [
            dma((2, 4, 3)), dma((2, 4, 3)),
            dma((2,)), dma((NY,)),
            dma((NY,)), dma((NY,)),
            dma((NY,)), dma((NY,)),
            dma((2, NY)), dma((2, NY)),
            dma((2, 2, NY)), dma((2, 2, NY)),
            dma((3, 2)), dma((3, 2)),
            dma((3, 2)), dma((3, 2)),
            dma((3, 2)), dma((3, 2)),
            dma((ROWS,)), dma((ROWS,)),
            dma((ROWS,)), dma((ROWS,)),
            dma(()),
        ],
        compiler_params=pltpu.CompilerParams(
            collective_id=0, has_side_effects=True, vmem_limit_bytes=40 * 1024 * 1024
        ),
    )(
        p1.reshape(2), p2.reshape(1), par.reshape(1), a, f1, two.reshape(B, B),
        pb.reshape(B, B), d1.reshape(2, B, B), d2.reshape(B, B),
    )
    return (
        inv1.transpose(1, 0, 2).reshape(one.shape),
        diag1.reshape(d1.shape),
        inv2.reshape(two.shape),
        pinv.reshape(pb.shape),
        diag2.reshape(d2.shape),
    )


def solution(mesh):
    placed = (
        P(None, "row", None, None, "col", None),
        P(None, "row", None, None, "col", None),
        P(None, "row", None, None, "col", None),
        P(None, "col", None, None),
        P(None, "col", None, None),
        P(None, "col", None, None),
        P(None, "row", None, "col"),
        P(None, "row", None, "col"),
        P(None, "col"),
    )
    return jax.shard_map(
        body,
        mesh=mesh,
        in_specs=placed,
        out_specs=(
            P(None, "row", None, None, "col", None),
            P(None, "col", None, None),
            P(None, "row", None, None, "col", None),
            P(None, "col", None, None),
            P(None, "col", None, None),
        ),
        check_vma=False,
    )
```

```python
import functools

import jax
import jax.numpy as jnp
from jax import lax
from jax.experimental import pallas as pl
from jax.experimental.pallas import tpu as pltpu
from jax.sharding import PartitionSpec as P

MESH = pl.DeviceIdType.MESH
B = 256
NY, NZ, NX = 4, 8, 4
ROWS = NY * NZ
SLICE = 2 * B // ROWS


def mm(a, b):
    return jnp.dot(a, b, preferred_element_type=jnp.float32)


def mm_t(a, b):
    return lax.dot_general(a, b, (((0,), (0,)), ((), ())), preferred_element_type=jnp.float32)


def kernel(
    p1_ref, p2_ref, par_ref, a_ref, f1_ref, f2_ref, pb_ref, d1_ref, d2_ref,
    inv1_ref, diag1_ref, inv2_ref, pinv_ref, diag2_ref,
    f_all, a_all, acc, e_send, e_recv, p_send, p_recv, g_send, g_recv,
    s0_part, s0_in, s0_mid, s0_mid_in, s0_out, s1_part, s1_in, s1_mid, s1_mid_in, s1_out,
    fs, fr, a1s, a1r, os, orr, xs, xr, ys, yr, cs, cr, es, er, ps, pr, gs, gr, ss, sr, own_sem,
):
    row, col = lax.axis_index("row"), lax.axis_index("col")
    y, z = row // NZ, row % NZ
    x, yl, core = col // 4, (col // 2) % 2, col % 2

    def remote(src, dst, ss, rs_, to_row, to_col):
        return pltpu.make_async_remote_copy(
            src_ref=src, dst_ref=dst, send_sem=ss, recv_sem=rs_,
            device_id=(to_row, to_col), device_id_type=MESH,
        )

    def z_mate(d):
        return y * NZ + lax.rem(z + d, NZ)

    def y_row(d):
        return lax.rem(y + d, NY) * NZ + z

    def col_of(x_, yl_, core_):
        return x_ * 4 + yl_ * 2 + core_

    y_mate = col_of(x, 1 - yl, core)
    c_mate = col_of(x, yl, 1 - core)
    across = col_of(x + 1 - 2 * lax.rem(x, 2), yl, core)
    outward = col_of(NX - 1 - x, yl, core)

    barrier = pltpu.get_barrier_semaphore()

    for mate in [z_mate(d) for d in range(1, NZ)] + [y_row(d) for d in range(1, NY)]:
        pl.semaphore_signal(barrier, inc=1, device_id=(mate, col), device_id_type=MESH)
    for mate in (across, outward, y_mate, c_mate):
        pl.semaphore_signal(barrier, inc=1, device_id=(row, mate), device_id_type=MESH)
    m0 = p1_ref[0].astype(jnp.float32)
    m1 = p1_ref[1].astype(jnp.float32)
    m2 = p2_ref[0].astype(jnp.float32)
    f_all[0, z] = f1_ref[0] * m0.astype(jnp.bfloat16)
    f_all[1, z] = f1_ref[1] * m1.astype(jnp.bfloat16)
    f_all[2, z] = f2_ref[...] * m2.astype(jnp.bfloat16)
    pl.semaphore_wait(barrier, NZ - 1 + NY - 1 + 4)

    up = y * NZ + lax.rem(z + 1, NZ)
    down = y * NZ + lax.rem(z + NZ - 1, NZ)
    half = B // 2

    def f_copies(step, k):
        up_slot = lax.rem(z + NZ - step, NZ)
        down_slot = lax.rem(z + step, NZ)
        if step < 3:
            u, d = f_all.at[k, up_slot], f_all.at[k, down_slot]
        else:
            u = f_all.at[k, up_slot, pl.ds(0, half)]
            d = f_all.at[k, down_slot, pl.ds(half, half)]
        return (
            remote(u, u, fs.at[0, step, k], fr.at[0, step, k], up, col),
            remote(d, d, fs.at[1, step, k], fr.at[1, step, k], down, col),
        )

    def f_step(step):
        for k in range(3):
            if step > 0:
                for copy in f_copies(step - 1, k):
                    copy.wait_recv()
            if step < 4:
                for copy in f_copies(step, k):
                    copy.start()

    slot = lax.rem(col, NZ)
    hold = lax.rem(y + x // 2 + 1, 2)
    near = lax.rem(x + 1 + hold, 2)

    def a1_copy(h):
        return remote(
            a_ref.at[h], a_all.at[slot, y], a1s.at[h], a1r.at[y], (2 * h + x // 2) * NZ + z, col
        )

    def own_copy(h):
        return pltpu.make_async_copy(a_ref.at[h], a_all.at[slot, y], own_sem)

    for h in range(2):
        target = 2 * h + x // 2

        @pl.when(target != y)
        def _():
            a1_copy(h).start()

        @pl.when(target == y)
        def _():
            own_copy(h).start()

    f_step(0)

    def chunk(far, yl_, core_, k):
        s = 1 - near if far else near
        return a_all.at[s * 4 + yl_ * 2 + core_, lax.rem(y + k, NY)]

    def o_copy(k):
        c = chunk(0, yl, core, k)
        return remote(c, c, os.at[k], orr.at[k], row, outward)

    def x_copy(k, far=0):
        c = chunk(far, yl, core, k)
        return remote(c, c, xs.at[k], xr.at[k], row, across)

    def y_copy(far, k, yl_):
        c = chunk(far, yl_, core, k)
        return remote(c, c, ys.at[far, k], yr.at[far, k], row, y_mate)

    def c_copy(far, other, k, core_):
        c = chunk(far, 1 - yl if other else yl, core_, k)
        return remote(c, c, cs.at[far, other, k], cr.at[far, other, k], row, c_mate)

    def stage_a(k):
        @pl.when(hold == 1)
        def _():
            if k == 0:
                own_copy(0).wait()
            else:
                other = lax.rem(y + k, NY)
                remote(
                    a_ref.at[0], a_all.at[slot, other], a1s.at[0], a1r.at[other], y_row(1), col
                ).wait_recv()
            o_copy(k).start()

        @pl.when(hold == 0)
        def _():
            o_copy(k).wait_recv()

        x_copy(k).start()
        y_copy(0, k, yl).start()
        c_copy(0, 0, k, core).start()

    def stage_b(k):
        x_copy(k, 1).wait_recv()
        y_copy(1, k, yl).start()
        c_copy(1, 0, k, core).start()

    def stage_c(k):
        for far in range(2):
            y_copy(far, k, 1 - yl).wait_recv()
            c_copy(far, 1, k, core).start()

    stage_a(0)
    stage_a(1)
    f_step(1)
    stage_b(0)
    stage_a(3)
    stage_c(0)
    stage_b(1)
    stage_a(2)
    f_step(2)
    stage_c(1)
    stage_b(3)
    stage_b(2)
    f_step(3)
    stage_c(3)
    stage_c(2)
    f_step(4)
    for k in (0, 1, 3, 2):
        for other in range(2):
            for far in range(2):
                c_copy(far, other, k, 1 - core).wait_recv()

    y_up = lax.rem(y + 1, NY)
    y_down = lax.rem(y + NY - 1, NY)
    row_up, row_down = y_up * NZ + z, y_down * NZ + z

    def product(y_, k):
        left = jnp.concatenate([a_all[i, y_] for i in range(NZ)], axis=1)
        return mm(left, f_all[k].reshape(NZ * B, B))

    def pair(send, recv, ss, rs_, k):
        return (
            remote(send.at[k, 0], recv.at[k, 0], ss.at[k, 0], rs_.at[k, 0], row_up, col),
            remote(send.at[k, 1], recv.at[k, 1], ss.at[k, 1], rs_.at[k, 1], row_down, col),
        )

    def early(k):
        return pair(e_send, e_recv, es, er, k)

    def plain(k):
        return pair(p_send, p_recv, ps, pr, k)

    def grown(k):
        return pair(g_send, g_recv, gs, gr, k)

    bf, f32 = jnp.bfloat16, jnp.float32

    def send_plain(k):
        part = product(y_up, k)
        acc[0, k] = part[:half]
        p_send[k, 0] = part[half:].astype(bf)
        plain(k)[0].start()
        part = product(y_down, k)
        acc[1, k] = part[half:]
        p_send[k, 1] = part[:half].astype(bf)
        plain(k)[1].start()

    def send_grown(k):
        for way in range(2):
            early(k)[way].wait_recv()
            g_send[k, way] = (acc[way, k] + e_recv[k, way].astype(f32)).astype(bf)
            grown(k)[way].start()

    def total(k):
        for way in range(2):
            plain(k)[way].wait_recv()
            grown(k)[way].wait_recv()
        top = acc[2, k] + (g_recv[k, 0].astype(f32) + p_recv[k, 1].astype(f32))
        bottom = acc[3, k] + (p_recv[k, 0].astype(f32) + g_recv[k, 1].astype(f32))
        return jnp.concatenate([top, bottom], axis=0)

    for k in range(3):
        part = product(lax.rem(y + 2, NY), k).astype(bf)
        e_send[k, 0] = part[:half]
        e_send[k, 1] = part[half:]
        for copy in early(k):
            copy.start()
    send_plain(0)
    send_plain(1)
    send_grown(0)
    send_grown(1)
    send_plain(2)
    send_grown(2)
    for k in range(3):
        part = product(y, k)
        acc[2, k] = part[:half]
        acc[3, k] = part[half:]

    def over_z(stage, src, dst):
        return [
            remote(src(d), dst(d), ss.at[stage, d], sr.at[stage, d], z_mate(d), col) for d in range(1, NZ)
        ]

    def over_y(stage, src, dst):
        return [
            remote(src(d), dst(d), ss.at[stage, d], sr.at[stage, d], y_row(d), col) for d in range(1, NY)
        ]

    def z_at(d):
        return lax.rem(z + d, NZ)

    def y_at(d):
        return lax.rem(y + d, NY)

    stages = (
        lambda: over_z(0, lambda d: s0_part.at[z_at(d)], lambda d: s0_in.at[d]),
        lambda: over_y(1, lambda d: s1_part.at[y_at(d)], lambda d: s1_in.at[d]),
        lambda: over_y(2, lambda d: s0_mid.at[y_at(d)], lambda d: s0_mid_in.at[d]),
        lambda: over_z(3, lambda d: s1_mid.at[z_at(d)], lambda d: s1_mid_in.at[d]),
        lambda: over_y(4, lambda d: s0_out.at[z, y], lambda d: s0_out.at[z, y]),
        lambda: over_z(5, lambda d: s1_out.at[y, z], lambda d: s1_out.at[y, z]),
        lambda: over_z(6, lambda d: s0_out.at[z], lambda d: s0_out.at[z]),
        lambda: over_y(7, lambda d: s1_out.at[y], lambda d: s1_out.at[y]),
    )

    def start(stage):
        for copy in stages[stage]():
            copy.start()

    def arrived(stage):
        for copy in stages[stage]():
            copy.wait_recv()

    def added(ref):
        return jnp.sum(ref[...].astype(f32), axis=0).astype(bf)

    second = par_ref[0] >= 16
    inv_a = (-total(0) * m0).astype(bf)
    inv_b = (-total(1) * m1).astype(bf)
    s0_part[pl.ds(0, NZ // 2)] = mm_t(f_all[0, z], inv_a).astype(bf).reshape(NZ // 2, NY * SLICE, B)
    s0_part[pl.ds(NZ // 2, NZ // 2)] = mm_t(f_all[1, z], inv_b).astype(bf).reshape(NZ // 2, NY * SLICE, B)
    start(0)
    s0_in[0] = s0_part[z]
    parent_cols = jnp.where(second, inv_b, inv_a)
    pb = pb_ref[...]
    side = mm(parent_cols, pb)
    s1_part[pl.ds(0, NY // 2)] = mm_t(parent_cols, f_all[2, z]).astype(bf).reshape(NY // 2, NZ * SLICE, B)
    inv_c = (-(total(2) + side) * m2).astype(bf)
    s1_part[pl.ds(NY // 2, NY // 2)] = mm_t(f_all[2, z], inv_c).astype(bf).reshape(NY // 2, NZ * SLICE, B)
    start(1)
    s1_in[0] = s1_part[y]
    inv1_ref[0] = inv_a
    inv1_ref[1] = inv_b
    inv2_ref[...] = inv_c
    arrived(0)
    s0_mid[...] = added(s0_in).reshape(NY, SLICE, B)
    start(2)
    s0_mid_in[0] = s0_mid[y]
    arrived(1)
    s1_mid[...] = added(s1_in).reshape(NZ, SLICE, B)
    start(3)
    s1_mid_in[0] = s1_mid[z]
    arrived(2)
    s0_out[z, y] = added(s0_mid_in)
    start(4)
    arrived(3)
    s1_out[y, z] = added(s1_mid_in)
    start(5)
    arrived(4)
    start(6)
    arrived(5)
    start(7)
    arrived(6)
    diag_sum = s0_out[...].reshape(2, B, B).astype(f32)
    diag_a = d1_ref[0] - diag_sum[0]
    diag_b = d1_ref[1] - diag_sum[1]
    diag1_ref[0] = diag_a
    diag1_ref[1] = diag_b
    parent_diag = jnp.where(second, diag_b, diag_a).astype(bf)
    ahead = mm(parent_diag, pb)
    arrived(7)
    other_sum = s1_out[...].reshape(2, B, B).astype(f32)
    pinv = (-(ahead + other_sum[0])).astype(bf)
    pinv_ref[...] = pinv
    diag2_ref[...] = d2_ref[...] - (other_sum[1] + mm_t(pb, pinv))

    for k in range(3):
        for step in range(4):
            for copy in f_copies(step, k):
                copy.wait_send()
        for copies in (early(k), plain(k), grown(k)):
            for copy in copies:
                copy.wait_send()
    for h in range(2):

        @pl.when(2 * h + x // 2 != y)
        def _():
            a1_copy(h).wait_send()

    @pl.when(hold == 1)
    def _():
        for k in range(NY):
            o_copy(k).wait_send()

    for k in range(NY):
        x_copy(k).wait_send()
        for far in range(2):
            y_copy(far, k, yl).wait_send()
            for other in range(2):
                c_copy(far, other, k, core).wait_send()
    for stage in stages:
        for copy in stage():
            copy.wait_send()


def body(anc, one, two, pb, d1, d2, p1, p2, par):
    a = anc.reshape(B, 2, B).transpose(1, 0, 2)
    f1 = one.reshape(B, 2, B).transpose(1, 0, 2)
    vmem = pl.BlockSpec(memory_space=pltpu.VMEM)
    smem = pl.BlockSpec(memory_space=pltpu.SMEM)
    dma = pltpu.SemaphoreType.DMA
    bf, f32 = jnp.bfloat16, jnp.float32
    inv1, diag1, inv2, pinv, diag2 = pl.pallas_call(
        kernel,
        out_shape=(
            jax.ShapeDtypeStruct((2, B, B), bf),
            jax.ShapeDtypeStruct((2, B, B), f32),
            jax.ShapeDtypeStruct((B, B), bf),
            jax.ShapeDtypeStruct((B, B), bf),
            jax.ShapeDtypeStruct((B, B), f32),
        ),
        in_specs=[smem] * 3 + [vmem] * 6,
        out_specs=(vmem,) * 5,
        scratch_shapes=[
            pltpu.VMEM((3, NZ, B, B), bf),
            pltpu.VMEM((NZ, NY, B, B), bf),
            pltpu.VMEM((4, 3, B // 2, B), f32),
        ]
        + [pltpu.VMEM((3, 2, B // 2, B), bf)] * 6
        + [
            pltpu.VMEM((NZ, NY * SLICE, B), bf), pltpu.VMEM((NZ, NY * SLICE, B), bf),
            pltpu.VMEM((NY, SLICE, B), bf), pltpu.VMEM((NY, SLICE, B), bf),
            pltpu.VMEM((NZ, NY, SLICE, B), bf),
            pltpu.VMEM((NY, NZ * SLICE, B), bf), pltpu.VMEM((NY, NZ * SLICE, B), bf),
            pltpu.VMEM((NZ, SLICE, B), bf), pltpu.VMEM((NZ, SLICE, B), bf),
            pltpu.VMEM((NY, NZ, SLICE, B), bf),
        ]
        + [
            dma((2, 4, 3)), dma((2, 4, 3)),
            dma((2,)), dma((NY,)),
            dma((NY,)), dma((NY,)),
            dma((NY,)), dma((NY,)),
            dma((2, NY)), dma((2, NY)),
            dma((2, 2, NY)), dma((2, 2, NY)),
            dma((3, 2)), dma((3, 2)),
            dma((3, 2)), dma((3, 2)),
            dma((3, 2)), dma((3, 2)),
            dma((8, NZ)), dma((8, NZ)),
            dma(()),
        ],
        compiler_params=pltpu.CompilerParams(
            collective_id=0, has_side_effects=True, vmem_limit_bytes=40 * 1024 * 1024
        ),
    )(
        p1.reshape(2), p2.reshape(1), par.reshape(1), a, f1, two.reshape(B, B),
        pb.reshape(B, B), d1.reshape(2, B, B), d2.reshape(B, B),
    )
    return (
        inv1.transpose(1, 0, 2).reshape(one.shape),
        diag1.reshape(d1.shape),
        inv2.reshape(two.shape),
        pinv.reshape(pb.shape),
        diag2.reshape(d2.shape),
    )


def solution(mesh):
    placed = (
        P(None, "row", None, None, "col", None),
        P(None, "row", None, None, "col", None),
        P(None, "row", None, None, "col", None),
        P(None, "col", None, None),
        P(None, "col", None, None),
        P(None, "col", None, None),
        P(None, "row", None, "col"),
        P(None, "row", None, "col"),
        P(None, "col"),
    )
    return jax.shard_map(
        body,
        mesh=mesh,
        in_specs=placed,
        out_specs=(
            P(None, "row", None, None, "col", None),
            P(None, "col", None, None),
            P(None, "row", None, None, "col", None),
            P(None, "col", None, None),
            P(None, "col", None, None),
        ),
        check_vma=False,
    )
```

```python
import functools

import jax
import jax.numpy as jnp
from jax import lax
from jax.experimental import pallas as pl
from jax.experimental.pallas import tpu as pltpu
from jax.sharding import PartitionSpec as P

MESH = pl.DeviceIdType.MESH
B = 256
NY, NZ, NX = 4, 8, 4
SLICE = B // NZ


def mm(a, b):
    return jnp.dot(a, b, preferred_element_type=jnp.float32)


def mm_t(a, b):
    return lax.dot_general(a, b, (((0,), (0,)), ((), ())), preferred_element_type=jnp.float32)


def kernel(
    p1_ref, p2_ref, par_ref, a_ref, f1_ref, f2_ref, pb_ref, d1_ref, d2_ref,
    inv1_ref, diag1_ref, inv2_ref, pinv_ref, diag2_ref,
    f_all, a_all, acc, e_send, e_recv, p_send, p_recv, g_send, g_recv,
    s0_part, s0_in, s0_mid, s0_out, s1_part, s1_in, s1_mid, s1_out,
    fs, fr, a1s, a1r, os, orr, xs, xr, ys, yr, cs, cr, es, er, ps, pr, gs, gr, ss, sr, own_sem,
):
    row, col = lax.axis_index("row"), lax.axis_index("col")
    y, z = row // NZ, row % NZ
    x, yl, core = col // 4, (col // 2) % 2, col % 2

    def remote(src, dst, ss, rs_, to_row, to_col):
        return pltpu.make_async_remote_copy(
            src_ref=src, dst_ref=dst, send_sem=ss, recv_sem=rs_,
            device_id=(to_row, to_col), device_id_type=MESH,
        )

    def z_mate(d):
        return y * NZ + lax.rem(z + d, NZ)

    def y_row(d):
        return lax.rem(y + d, NY) * NZ + z

    def col_of(x_, yl_, core_):
        return x_ * 4 + yl_ * 2 + core_

    y_mate = col_of(x, 1 - yl, core)
    c_mate = col_of(x, yl, 1 - core)
    across = col_of(x + 1 - 2 * lax.rem(x, 2), yl, core)
    outward = col_of(NX - 1 - x, yl, core)

    barrier = pltpu.get_barrier_semaphore()

    for mate in [z_mate(d) for d in range(1, NZ)] + [y_row(d) for d in range(1, NY)]:
        pl.semaphore_signal(barrier, inc=1, device_id=(mate, col), device_id_type=MESH)
    for mate in (across, outward, y_mate, c_mate):
        pl.semaphore_signal(barrier, inc=1, device_id=(row, mate), device_id_type=MESH)
    m0 = p1_ref[0].astype(jnp.float32)
    m1 = p1_ref[1].astype(jnp.float32)
    m2 = p2_ref[0].astype(jnp.float32)
    f_all[0, z] = f1_ref[0] * m0.astype(jnp.bfloat16)
    f_all[1, z] = f1_ref[1] * m1.astype(jnp.bfloat16)
    f_all[2, z] = f2_ref[...] * m2.astype(jnp.bfloat16)
    pl.semaphore_wait(barrier, NZ - 1 + NY - 1 + 4)

    up = y * NZ + lax.rem(z + 1, NZ)
    down = y * NZ + lax.rem(z + NZ - 1, NZ)
    half = B // 2

    def f_copies(step, k):
        up_slot = lax.rem(z + NZ - step, NZ)
        down_slot = lax.rem(z + step, NZ)
        if step < 3:
            u, d = f_all.at[k, up_slot], f_all.at[k, down_slot]
        else:
            u = f_all.at[k, up_slot, pl.ds(0, half)]
            d = f_all.at[k, down_slot, pl.ds(half, half)]
        return (
            remote(u, u, fs.at[0, step, k], fr.at[0, step, k], up, col),
            remote(d, d, fs.at[1, step, k], fr.at[1, step, k], down, col),
        )

    def f_step(k, step):
        if step > 0:
            for copy in f_copies(step - 1, k):
                copy.wait_recv()
        if step < 4:
            for copy in f_copies(step, k):
                copy.start()

    slot = lax.rem(col, NZ)
    hold = lax.rem(y + x // 2 + 1, 2)
    near = lax.rem(x + 1 + hold, 2)

    def a1_copy(h):
        return remote(
            a_ref.at[h], a_all.at[slot, y], a1s.at[h], a1r.at[y], (2 * h + x // 2) * NZ + z, col
        )

    def own_copy(h):
        return pltpu.make_async_copy(a_ref.at[h], a_all.at[slot, y], own_sem)

    for h in range(2):
        target = 2 * h + x // 2

        @pl.when(target != y)
        def _():
            a1_copy(h).start()

        @pl.when(target == y)
        def _():
            own_copy(h).start()

    def chunk(far, yl_, core_, k):
        s = 1 - near if far else near
        return a_all.at[s * 4 + yl_ * 2 + core_, lax.rem(y + k, NY)]

    def y_copy(k, yl_):
        c = chunk(0, yl_, core, k)
        return remote(c, c, ys.at[k], yr.at[k], row, y_mate)

    def o_copy(other, k):
        c = chunk(0, 1 - yl if other else yl, core, k)
        return remote(c, c, os.at[other, k], orr.at[other, k], row, outward)

    def x_copy(other, k, far=0):
        c = chunk(far, 1 - yl if other else yl, core, k)
        return remote(c, c, xs.at[other, k], xr.at[other, k], row, across)

    def c_copy(far, other, k, core_):
        c = chunk(far, 1 - yl if other else yl, core_, k)
        return remote(c, c, cs.at[far, other, k], cr.at[far, other, k], row, c_mate)

    def near_own(k):
        @pl.when(hold == 1)
        def _():
            if k == 0:
                own_copy(0).wait()
            else:
                other = lax.rem(y + k, NY)
                remote(
                    a_ref.at[0], a_all.at[slot, other], a1s.at[0], a1r.at[other], y_row(1), col
                ).wait_recv()
            y_copy(k, yl).start()
            o_copy(0, k).start()

        @pl.when(hold == 0)
        def _():
            o_copy(0, k).wait_recv()

        x_copy(0, k).start()
        c_copy(0, 0, k, core).start()

    def near_other(k):
        @pl.when(hold == 1)
        def _():
            y_copy(k, 1 - yl).wait_recv()
            o_copy(1, k).start()

        @pl.when(hold == 0)
        def _():
            o_copy(1, k).wait_recv()

        x_copy(1, k).start()
        c_copy(0, 1, k, core).start()

    def far_both(k):
        for other in range(2):
            x_copy(other, k, 1).wait_recv()
            c_copy(1, other, k, core).start()

    def whole(k):
        for far in range(2):
            for other in range(2):
                c_copy(far, other, k, 1 - core).wait_recv()

    y_up = lax.rem(y + 1, NY)
    y_down = lax.rem(y + NY - 1, NY)
    row_up, row_down = y_up * NZ + z, y_down * NZ + z

    def product(y_, k):
        left = jnp.concatenate([a_all[i, y_] for i in range(NZ)], axis=1)
        return mm(left, f_all[k].reshape(NZ * B, B))

    def pair(send, recv, ss, rs_, k):
        return (
            remote(send.at[k, 0], recv.at[k, 0], ss.at[k, 0], rs_.at[k, 0], row_up, col),
            remote(send.at[k, 1], recv.at[k, 1], ss.at[k, 1], rs_.at[k, 1], row_down, col),
        )

    def early(k):
        return pair(e_send, e_recv, es, er, k)

    def plain(k):
        return pair(p_send, p_recv, ps, pr, k)

    def grown(k):
        return pair(g_send, g_recv, gs, gr, k)

    bf, f32 = jnp.bfloat16, jnp.float32

    def send_early(k):
        part = product(lax.rem(y + 2, NY), k).astype(bf)
        e_send[k, 0] = part[:half]
        e_send[k, 1] = part[half:]
        for copy in early(k):
            copy.start()

    def send_up(k):
        part = product(y_up, k)
        acc[0, k] = part[:half]
        p_send[k, 0] = part[half:].astype(bf)
        plain(k)[0].start()

    def send_down(k):
        part = product(y_down, k)
        acc[1, k] = part[half:]
        p_send[k, 1] = part[:half].astype(bf)
        plain(k)[1].start()

    def own(k):
        part = product(y, k)
        acc[2, k] = part[:half]
        acc[3, k] = part[half:]

    def send_grown(k):
        for way in range(2):
            early(k)[way].wait_recv()
            g_send[k, way] = (acc[way, k] + e_recv[k, way].astype(f32)).astype(bf)
            grown(k)[way].start()

    def total(k):
        for way in range(2):
            plain(k)[way].wait_recv()
            grown(k)[way].wait_recv()
        top = acc[2, k] + (g_recv[k, 0].astype(f32) + p_recv[k, 1].astype(f32))
        bottom = acc[3, k] + (p_recv[k, 0].astype(f32) + g_recv[k, 1].astype(f32))
        return jnp.concatenate([top, bottom], axis=0)

    f_step(0, 0)
    f_step(1, 0)
    near_own(0)
    f_step(0, 1)
    near_other(0)
    f_step(1, 1)
    near_own(2)
    far_both(0)
    f_step(0, 2)
    near_own(1)
    near_other(2)
    f_step(1, 2)
    near_own(3)
    far_both(2)
    near_other(1)
    f_step(0, 3)
    f_step(2, 0)
    f_step(1, 3)
    near_other(3)
    far_both(1)
    whole(2)
    f_step(2, 1)
    f_step(0, 4)
    send_early(0)
    f_step(1, 4)
    send_early(1)
    far_both(3)
    whole(1)
    f_step(2, 2)
    send_up(0)
    send_up(1)
    whole(3)
    send_down(0)
    send_down(1)
    f_step(2, 3)
    send_grown(0)
    send_grown(1)
    whole(0)
    own(0)
    own(1)
    f_step(2, 4)
    send_early(2)
    send_up(2)
    send_down(2)
    own(2)

    def over_z(stage, src, dst):
        return [
            remote(src(d), dst(d), ss.at[stage, d], sr.at[stage, d], z_mate(d), col) for d in range(1, NZ)
        ]

    def over_y(stage, src, dst):
        return [
            remote(src(d), dst(d), ss.at[stage, d], sr.at[stage, d], y_row(d), col) for d in range(1, NY)
        ]

    def z_at(d):
        return lax.rem(z + d, NZ)

    stages = (
        lambda: over_z(0, lambda d: s0_part.at[z_at(d)], lambda d: s0_in.at[d]),
        lambda: over_z(1, lambda d: s1_part.at[z_at(d)], lambda d: s1_in.at[d]),
        lambda: over_y(2, lambda d: s0_mid.at[y], lambda d: s0_mid.at[y]),
        lambda: over_y(3, lambda d: s1_mid.at[y], lambda d: s1_mid.at[y]),
        lambda: over_z(4, lambda d: s0_out.at[z], lambda d: s0_out.at[z]),
        lambda: over_z(5, lambda d: s1_out.at[z], lambda d: s1_out.at[z]),
    )

    def start(stage):
        for copy in stages[stage]():
            copy.start()

    def arrived(stage):
        for copy in stages[stage]():
            copy.wait_recv()

    def added(ref):
        return jnp.sum(ref[...].astype(f32), axis=0).astype(bf)

    second = par_ref[0] >= 16
    inv_a = (-total(0) * m0).astype(bf)
    inv_b = (-total(1) * m1).astype(bf)
    parent_cols = jnp.where(second, inv_b, inv_a)
    level_one = jnp.concatenate(
        [mm_t(f_all[0, z], inv_a), mm_t(f_all[1, z], inv_b), mm_t(parent_cols, f_all[2, z])], axis=0
    )
    s0_part[...] = level_one.astype(bf).reshape(NZ, 3 * SLICE, B)
    start(0)
    send_grown(2)
    s0_in[0] = s0_part[z]
    pb = pb_ref[...]
    side = mm(parent_cols, pb)
    inv1_ref[0] = inv_a
    inv1_ref[1] = inv_b
    inv_c = (-(total(2) + side) * m2).astype(bf)
    s1_part[...] = mm_t(f_all[2, z], inv_c).astype(bf).reshape(NZ, SLICE, B)
    start(1)
    s1_in[0] = s1_part[z]
    inv2_ref[...] = inv_c
    arrived(0)
    s0_mid[y] = added(s0_in)
    start(2)
    arrived(1)
    s1_mid[y] = added(s1_in)
    start(3)
    arrived(2)
    s0_out[z] = added(s0_mid)
    start(4)
    arrived(3)
    s1_out[z] = added(s1_mid)
    start(5)
    arrived(4)
    sums = s0_out[...].reshape(3, B, B).astype(f32)
    diag_a = d1_ref[0] - sums[0]
    diag_b = d1_ref[1] - sums[1]
    diag1_ref[0] = diag_a
    diag1_ref[1] = diag_b
    parent_diag = jnp.where(second, diag_b, diag_a).astype(bf)
    pinv = (-(mm(parent_diag, pb) + sums[2])).astype(bf)
    pinv_ref[...] = pinv
    ahead = d2_ref[...] - mm_t(pb, pinv)
    arrived(5)
    diag2_ref[...] = ahead - s1_out[...].reshape(B, B).astype(f32)

    for k in range(3):
        for step in range(4):
            for copy in f_copies(step, k):
                copy.wait_send()
        for copies in (early(k), plain(k), grown(k)):
            for copy in copies:
                copy.wait_send()
    for h in range(2):

        @pl.when(2 * h + x // 2 != y)
        def _():
            a1_copy(h).wait_send()

    @pl.when(hold == 1)
    def _():
        for k in range(NY):
            y_copy(k, yl).wait_send()
            for other in range(2):
                o_copy(other, k).wait_send()

    for k in range(NY):
        for other in range(2):
            x_copy(other, k).wait_send()
            for far in range(2):
                c_copy(far, other, k, core).wait_send()
    for stage in stages:
        for copy in stage():
            copy.wait_send()


def body(anc, one, two, pb, d1, d2, p1, p2, par):
    a = anc.reshape(B, 2, B).transpose(1, 0, 2)
    f1 = one.reshape(B, 2, B).transpose(1, 0, 2)
    vmem = pl.BlockSpec(memory_space=pltpu.VMEM)
    smem = pl.BlockSpec(memory_space=pltpu.SMEM)
    dma = pltpu.SemaphoreType.DMA
    bf, f32 = jnp.bfloat16, jnp.float32
    inv1, diag1, inv2, pinv, diag2 = pl.pallas_call(
        kernel,
        out_shape=(
            jax.ShapeDtypeStruct((2, B, B), bf),
            jax.ShapeDtypeStruct((2, B, B), f32),
            jax.ShapeDtypeStruct((B, B), bf),
            jax.ShapeDtypeStruct((B, B), bf),
            jax.ShapeDtypeStruct((B, B), f32),
        ),
        in_specs=[smem] * 3 + [vmem] * 6,
        out_specs=(vmem,) * 5,
        scratch_shapes=[
            pltpu.VMEM((3, NZ, B, B), bf),
            pltpu.VMEM((NZ, NY, B, B), bf),
            pltpu.VMEM((4, 3, B // 2, B), f32),
        ]
        + [pltpu.VMEM((3, 2, B // 2, B), bf)] * 6
        + [
            pltpu.VMEM((NZ, 3 * SLICE, B), bf), pltpu.VMEM((NZ, 3 * SLICE, B), bf),
            pltpu.VMEM((NY, 3 * SLICE, B), bf), pltpu.VMEM((NZ, 3 * SLICE, B), bf),
            pltpu.VMEM((NZ, SLICE, B), bf), pltpu.VMEM((NZ, SLICE, B), bf),
            pltpu.VMEM((NY, SLICE, B), bf), pltpu.VMEM((NZ, SLICE, B), bf),
        ]
        + [
            dma((2, 4, 3)), dma((2, 4, 3)),
            dma((2,)), dma((NY,)),
            dma((2, NY)), dma((2, NY)),
            dma((2, NY)), dma((2, NY)),
            dma((NY,)), dma((NY,)),
            dma((2, 2, NY)), dma((2, 2, NY)),
            dma((3, 2)), dma((3, 2)),
            dma((3, 2)), dma((3, 2)),
            dma((3, 2)), dma((3, 2)),
            dma((6, NZ)), dma((6, NZ)),
            dma(()),
        ],
        compiler_params=pltpu.CompilerParams(
            collective_id=0, has_side_effects=True, vmem_limit_bytes=40 * 1024 * 1024
        ),
    )(
        p1.reshape(2), p2.reshape(1), par.reshape(1), a, f1, two.reshape(B, B),
        pb.reshape(B, B), d1.reshape(2, B, B), d2.reshape(B, B),
    )
    return (
        inv1.transpose(1, 0, 2).reshape(one.shape),
        diag1.reshape(d1.shape),
        inv2.reshape(two.shape),
        pinv.reshape(pb.shape),
        diag2.reshape(d2.shape),
    )


def solution(mesh):
    placed = (
        P(None, "row", None, None, "col", None),
        P(None, "row", None, None, "col", None),
        P(None, "row", None, None, "col", None),
        P(None, "col", None, None),
        P(None, "col", None, None),
        P(None, "col", None, None),
        P(None, "row", None, "col"),
        P(None, "row", None, "col"),
        P(None, "col"),
    )
    return jax.shard_map(
        body,
        mesh=mesh,
        in_specs=placed,
        out_specs=(
            P(None, "row", None, None, "col", None),
            P(None, "col", None, None),
            P(None, "row", None, None, "col", None),
            P(None, "col", None, None),
            P(None, "col", None, None),
        ),
        check_vma=False,
    )
```

```python
import functools

import jax
import jax.numpy as jnp
from jax import lax
from jax.experimental import pallas as pl
from jax.experimental.pallas import tpu as pltpu
from jax.sharding import PartitionSpec as P

MESH = pl.DeviceIdType.MESH
B = 256
NY, NZ, NX = 4, 8, 4
SLICE = B // NZ


def mm(a, b):
    return jnp.dot(a, b, preferred_element_type=jnp.float32)


def mm_t(a, b):
    return lax.dot_general(a, b, (((0,), (0,)), ((), ())), preferred_element_type=jnp.float32)


def kernel(
    p1_ref, p2_ref, par_ref, a_ref, f1_ref, f2_ref, pb_ref, d1_ref, d2_ref,
    inv1_ref, diag1_ref, inv2_ref, pinv_ref, diag2_ref,
    f_all, a_all, acc, e_send, e_recv, p_send, p_recv, g_send, g_recv,
    s0_part, s0_in, s0_mid, s0_out, s1_part, s1_in, s1_mid, s1_out,
    fs, fr, a1s, a1r, os, orr, xs, xr, ys, yr, cs, cr, es, er, ps, pr, gs, gr, ss, sr, own_sem,
):
    row, col = lax.axis_index("row"), lax.axis_index("col")
    y, z = row // NZ, row % NZ
    x, yl, core = col // 4, (col // 2) % 2, col % 2

    def remote(src, dst, ss, rs_, to_row, to_col):
        return pltpu.make_async_remote_copy(
            src_ref=src, dst_ref=dst, send_sem=ss, recv_sem=rs_,
            device_id=(to_row, to_col), device_id_type=MESH,
        )

    def z_mate(d):
        return y * NZ + lax.rem(z + d, NZ)

    def y_row(d):
        return lax.rem(y + d, NY) * NZ + z

    def col_of(x_, yl_, core_):
        return x_ * 4 + yl_ * 2 + core_

    y_mate = col_of(x, 1 - yl, core)
    c_mate = col_of(x, yl, 1 - core)
    across = col_of(x + 1 - 2 * lax.rem(x, 2), yl, core)
    outward = col_of(NX - 1 - x, yl, core)

    barrier = pltpu.get_barrier_semaphore()

    for mate in [z_mate(d) for d in range(1, NZ)] + [y_row(d) for d in range(1, NY)]:
        pl.semaphore_signal(barrier, inc=1, device_id=(mate, col), device_id_type=MESH)
    for mate in (across, outward, y_mate, c_mate):
        pl.semaphore_signal(barrier, inc=1, device_id=(row, mate), device_id_type=MESH)
    m0 = p1_ref[0].astype(jnp.float32)
    m1 = p1_ref[1].astype(jnp.float32)
    m2 = p2_ref[0].astype(jnp.float32)
    f_all[0, z] = f1_ref[0] * m0.astype(jnp.bfloat16)
    f_all[1, z] = f1_ref[1] * m1.astype(jnp.bfloat16)
    f_all[2, z] = f2_ref[...] * m2.astype(jnp.bfloat16)
    pl.semaphore_wait(barrier, NZ - 1 + NY - 1 + 4)

    up = y * NZ + lax.rem(z + 1, NZ)
    down = y * NZ + lax.rem(z + NZ - 1, NZ)
    half = B // 2

    def f_copies(stream, step):
        k = min(stream, 2)
        top, bottom = pl.ds(0, half), pl.ds(half, half)
        if stream < 2:
            ups, downs = (pl.ds(0, B), pl.ds(0, B)) if step < 3 else (top, bottom)
        else:
            ups = downs = top if stream == 2 else bottom
        u = f_all.at[k, lax.rem(z + NZ - step, NZ), ups]
        d = f_all.at[k, lax.rem(z + step, NZ), downs]
        copies = []
        if step < 3 or stream != 3:
            copies.append(remote(u, u, fs.at[0, step, stream], fr.at[0, step, stream], up, col))
        if step < 3 or stream != 2:
            copies.append(remote(d, d, fs.at[1, step, stream], fr.at[1, step, stream], down, col))
        return copies

    def f_step(stream, step):
        if step > 0:
            for copy in f_copies(stream, step - 1):
                copy.wait_recv()
        if step < 4:
            for copy in f_copies(stream, step):
                copy.start()

    slot = lax.rem(col, NZ)
    hold = lax.rem(y + x // 2 + 1, 2)
    near = lax.rem(x + 1 + hold, 2)

    def a1_copy(h):
        return remote(
            a_ref.at[h], a_all.at[slot, y], a1s.at[h], a1r.at[y], (2 * h + x // 2) * NZ + z, col
        )

    def own_copy(h):
        return pltpu.make_async_copy(a_ref.at[h], a_all.at[slot, y], own_sem)

    for h in range(2):
        target = 2 * h + x // 2

        @pl.when(target != y)
        def _():
            a1_copy(h).start()

        @pl.when(target == y)
        def _():
            own_copy(h).start()

    def chunk(far, yl_, core_, k):
        s = 1 - near if far else near
        return a_all.at[s * 4 + yl_ * 2 + core_, lax.rem(y + k, NY)]

    def y_copy(k, yl_):
        c = chunk(0, yl_, core, k)
        return remote(c, c, ys.at[k], yr.at[k], row, y_mate)

    def o_copy(other, k):
        c = chunk(0, 1 - yl if other else yl, core, k)
        return remote(c, c, os.at[other, k], orr.at[other, k], row, outward)

    def x_copy(other, k, far=0):
        c = chunk(far, 1 - yl if other else yl, core, k)
        return remote(c, c, xs.at[other, k], xr.at[other, k], row, across)

    def c_copy(far, other, k, core_):
        c = chunk(far, 1 - yl if other else yl, core_, k)
        return remote(c, c, cs.at[far, other, k], cr.at[far, other, k], row, c_mate)

    def near_own(k):
        @pl.when(hold == 1)
        def _():
            if k == 0:
                own_copy(0).wait()
            else:
                other = lax.rem(y + k, NY)
                remote(
                    a_ref.at[0], a_all.at[slot, other], a1s.at[0], a1r.at[other], y_row(1), col
                ).wait_recv()
            y_copy(k, yl).start()
            o_copy(0, k).start()

        @pl.when(hold == 0)
        def _():
            o_copy(0, k).wait_recv()

        x_copy(0, k).start()
        c_copy(0, 0, k, core).start()

    def near_other(k):
        @pl.when(hold == 1)
        def _():
            y_copy(k, 1 - yl).wait_recv()
            o_copy(1, k).start()

        @pl.when(hold == 0)
        def _():
            o_copy(1, k).wait_recv()

        x_copy(1, k).start()
        c_copy(0, 1, k, core).start()

    def far_both(k):
        for other in range(2):
            x_copy(other, k, 1).wait_recv()
            c_copy(1, other, k, core).start()

    def whole(k):
        for far in range(2):
            for other in range(2):
                c_copy(far, other, k, 1 - core).wait_recv()

    y_up = lax.rem(y + 1, NY)
    y_down = lax.rem(y + NY - 1, NY)
    row_up, row_down = y_up * NZ + z, y_down * NZ + z

    def product(y_, k):
        left = jnp.concatenate([a_all[i, y_] for i in range(NZ)], axis=1)
        return mm(left, f_all[k].reshape(NZ * B, B))

    def pair(send, recv, ss, rs_, k):
        return (
            remote(send.at[k, 0], recv.at[k, 0], ss.at[k, 0], rs_.at[k, 0], row_up, col),
            remote(send.at[k, 1], recv.at[k, 1], ss.at[k, 1], rs_.at[k, 1], row_down, col),
        )

    def early(k):
        return pair(e_send, e_recv, es, er, k)

    def plain(k):
        return pair(p_send, p_recv, ps, pr, k)

    def grown(k):
        return pair(g_send, g_recv, gs, gr, k)

    bf, f32 = jnp.bfloat16, jnp.float32

    def send_early(k):
        part = product(lax.rem(y + 2, NY), k).astype(bf)
        e_send[k, 0] = part[:half]
        e_send[k, 1] = part[half:]
        for copy in early(k):
            copy.start()

    def send_up(k):
        part = product(y_up, k)
        acc[0, k] = part[:half]
        p_send[k, 0] = part[half:].astype(bf)
        plain(k)[0].start()

    def send_down(k):
        part = product(y_down, k)
        acc[1, k] = part[half:]
        p_send[k, 1] = part[:half].astype(bf)
        plain(k)[1].start()

    def own(k):
        part = product(y, k)
        acc[2, k] = part[:half]
        acc[3, k] = part[half:]

    def send_grown(k):
        for way in range(2):
            early(k)[way].wait_recv()
            g_send[k, way] = (acc[way, k] + e_recv[k, way].astype(f32)).astype(bf)
            grown(k)[way].start()

    def total(k):
        for way in range(2):
            plain(k)[way].wait_recv()
            grown(k)[way].wait_recv()
        top = acc[2, k] + (g_recv[k, 0].astype(f32) + p_recv[k, 1].astype(f32))
        bottom = acc[3, k] + (p_recv[k, 0].astype(f32) + g_recv[k, 1].astype(f32))
        return jnp.concatenate([top, bottom], axis=0)

    f_step(0, 0)
    f_step(1, 0)
    near_own(0)
    f_step(0, 1)
    f_step(1, 1)
    near_other(0)
    f_step(0, 2)
    near_own(2)
    f_step(1, 2)
    f_step(2, 0)
    far_both(0)
    near_own(1)
    near_other(2)
    f_step(0, 3)
    f_step(3, 0)
    f_step(1, 3)
    f_step(2, 1)
    near_own(3)
    far_both(2)
    near_other(1)
    f_step(3, 1)
    f_step(0, 4)
    f_step(2, 2)
    near_other(3)
    far_both(1)
    whole(2)
    send_early(0)
    f_step(1, 4)
    send_early(1)
    f_step(3, 2)
    f_step(2, 3)
    far_both(3)
    whole(1)
    send_up(0)
    send_up(1)
    whole(3)
    send_down(0)
    send_down(1)
    f_step(3, 3)
    send_grown(0)
    send_grown(1)
    f_step(2, 4)
    f_step(3, 4)
    send_early(2)
    send_up(2)
    send_down(2)
    whole(0)
    own(0)
    own(1)
    own(2)

    def over_z(stage, src, dst):
        return [
            remote(src(d), dst(d), ss.at[stage, d], sr.at[stage, d], z_mate(d), col) for d in range(1, NZ)
        ]

    def over_y(stage, src, dst):
        return [
            remote(src(d), dst(d), ss.at[stage, d], sr.at[stage, d], y_row(d), col) for d in range(1, NY)
        ]

    def z_at(d):
        return lax.rem(z + d, NZ)

    stages = (
        lambda: over_z(0, lambda d: s0_part.at[z_at(d)], lambda d: s0_in.at[d]),
        lambda: over_z(1, lambda d: s1_part.at[z_at(d)], lambda d: s1_in.at[d]),
        lambda: over_y(2, lambda d: s0_mid.at[y], lambda d: s0_mid.at[y]),
        lambda: over_y(3, lambda d: s1_mid.at[y], lambda d: s1_mid.at[y]),
        lambda: over_z(4, lambda d: s0_out.at[z], lambda d: s0_out.at[z]),
        lambda: over_z(5, lambda d: s1_out.at[z], lambda d: s1_out.at[z]),
    )

    def start(stage):
        for copy in stages[stage]():
            copy.start()

    def arrived(stage):
        for copy in stages[stage]():
            copy.wait_recv()

    def sent(stage):
        for copy in stages[stage]():
            copy.wait_send()

    def added(ref):
        return jnp.sum(ref[...].astype(f32), axis=0).astype(bf)

    second = par_ref[0] >= 16
    inv_a = (-total(0) * m0).astype(bf)
    inv_b = (-total(1) * m1).astype(bf)
    parent_cols = jnp.where(second, inv_b, inv_a)
    level_one = jnp.concatenate(
        [mm_t(f_all[0, z], inv_a), mm_t(f_all[1, z], inv_b), mm_t(parent_cols, f_all[2, z])], axis=0
    )
    s0_part[...] = level_one.astype(bf).reshape(NZ, 3 * SLICE, B)
    start(0)
    send_grown(2)
    s0_in[0] = s0_part[z]
    pb = pb_ref[...]
    side = mm(parent_cols, pb)
    inv1_ref[0] = inv_a
    inv1_ref[1] = inv_b
    inv_c = (-(total(2) + side) * m2).astype(bf)
    s1_part[...] = mm_t(f_all[2, z], inv_c).astype(bf).reshape(NZ, SLICE, B)
    start(1)
    s1_in[0] = s1_part[z]
    inv2_ref[...] = inv_c
    arrived(0)
    s0_mid[y] = added(s0_in)
    start(2)
    for stream in range(4):
        for step in range(4):
            for copy in f_copies(stream, step):
                copy.wait_send()
    for k in range(3):
        for copies in (early(k), plain(k), grown(k)):
            for copy in copies:
                copy.wait_send()
    for h in range(2):

        @pl.when(2 * h + x // 2 != y)
        def _():
            a1_copy(h).wait_send()

    @pl.when(hold == 1)
    def _():
        for k in range(NY):
            y_copy(k, yl).wait_send()
            for other in range(2):
                o_copy(other, k).wait_send()

    for k in range(NY):
        for other in range(2):
            x_copy(other, k).wait_send()
            for far in range(2):
                c_copy(far, other, k, core).wait_send()

    arrived(1)
    s1_mid[y] = added(s1_in)
    start(3)
    arrived(2)
    s0_out[z] = added(s0_mid)
    start(4)
    arrived(3)
    s1_out[z] = added(s1_mid)
    start(5)
    for stage in range(4):
        sent(stage)
    arrived(4)
    sums = s0_out[...].reshape(3, B, B).astype(f32)
    diag_a = d1_ref[0] - sums[0]
    diag_b = d1_ref[1] - sums[1]
    diag1_ref[0] = diag_a
    diag1_ref[1] = diag_b
    parent_diag = jnp.where(second, diag_b, diag_a).astype(bf)
    pinv = (-(mm(parent_diag, pb) + sums[2])).astype(bf)
    pinv_ref[...] = pinv
    ahead = d2_ref[...] - mm_t(pb, pinv)
    sent(4)
    arrived(5)
    diag2_ref[...] = ahead - s1_out[...].reshape(B, B).astype(f32)

    sent(5)


def body(anc, one, two, pb, d1, d2, p1, p2, par):
    a = anc.reshape(B, 2, B).transpose(1, 0, 2)
    f1 = one.reshape(B, 2, B).transpose(1, 0, 2)
    vmem = pl.BlockSpec(memory_space=pltpu.VMEM)
    smem = pl.BlockSpec(memory_space=pltpu.SMEM)
    dma = pltpu.SemaphoreType.DMA
    bf, f32 = jnp.bfloat16, jnp.float32
    inv1, diag1, inv2, pinv, diag2 = pl.pallas_call(
        kernel,
        out_shape=(
            jax.ShapeDtypeStruct((2, B, B), bf),
            jax.ShapeDtypeStruct((2, B, B), f32),
            jax.ShapeDtypeStruct((B, B), bf),
            jax.ShapeDtypeStruct((B, B), bf),
            jax.ShapeDtypeStruct((B, B), f32),
        ),
        in_specs=[smem] * 3 + [vmem] * 6,
        out_specs=(vmem,) * 5,
        scratch_shapes=[
            pltpu.VMEM((3, NZ, B, B), bf),
            pltpu.VMEM((NZ, NY, B, B), bf),
            pltpu.VMEM((4, 3, B // 2, B), f32),
        ]
        + [pltpu.VMEM((3, 2, B // 2, B), bf)] * 6
        + [
            pltpu.VMEM((NZ, 3 * SLICE, B), bf), pltpu.VMEM((NZ, 3 * SLICE, B), bf),
            pltpu.VMEM((NY, 3 * SLICE, B), bf), pltpu.VMEM((NZ, 3 * SLICE, B), bf),
            pltpu.VMEM((NZ, SLICE, B), bf), pltpu.VMEM((NZ, SLICE, B), bf),
            pltpu.VMEM((NY, SLICE, B), bf), pltpu.VMEM((NZ, SLICE, B), bf),
        ]
        + [
            dma((2, 4, 4)), dma((2, 4, 4)),
            dma((2,)), dma((NY,)),
            dma((2, NY)), dma((2, NY)),
            dma((2, NY)), dma((2, NY)),
            dma((NY,)), dma((NY,)),
            dma((2, 2, NY)), dma((2, 2, NY)),
            dma((3, 2)), dma((3, 2)),
            dma((3, 2)), dma((3, 2)),
            dma((3, 2)), dma((3, 2)),
            dma((6, NZ)), dma((6, NZ)),
            dma(()),
        ],
        compiler_params=pltpu.CompilerParams(
            collective_id=0, has_side_effects=True, vmem_limit_bytes=40 * 1024 * 1024
        ),
    )(
        p1.reshape(2), p2.reshape(1), par.reshape(1), a, f1, two.reshape(B, B),
        pb.reshape(B, B), d1.reshape(2, B, B), d2.reshape(B, B),
    )
    return (
        inv1.transpose(1, 0, 2).reshape(one.shape),
        diag1.reshape(d1.shape),
        inv2.reshape(two.shape),
        pinv.reshape(pb.shape),
        diag2.reshape(d2.shape),
    )


def solution(mesh):
    placed = (
        P(None, "row", None, None, "col", None),
        P(None, "row", None, None, "col", None),
        P(None, "row", None, None, "col", None),
        P(None, "col", None, None),
        P(None, "col", None, None),
        P(None, "col", None, None),
        P(None, "row", None, "col"),
        P(None, "row", None, "col"),
        P(None, "col"),
    )
    return jax.shard_map(
        body,
        mesh=mesh,
        in_specs=placed,
        out_specs=(
            P(None, "row", None, None, "col", None),
            P(None, "col", None, None),
            P(None, "row", None, None, "col", None),
            P(None, "col", None, None),
            P(None, "col", None, None),
        ),
        check_vma=False,
    )
```

```python
import functools

import jax
import jax.numpy as jnp
from jax import lax
from jax.experimental import pallas as pl
from jax.experimental.pallas import tpu as pltpu
from jax.sharding import PartitionSpec as P

MESH = pl.DeviceIdType.MESH
B = 256
NY, NZ, NX = 4, 8, 4
SLICE = B // NZ


def mm(a, b):
    return jnp.dot(a, b, preferred_element_type=jnp.float32)


def mm_t(a, b):
    return lax.dot_general(a, b, (((0,), (0,)), ((), ())), preferred_element_type=jnp.float32)


def kernel(
    p1_ref, p2_ref, par_ref, a_ref, f1_ref, f2_ref, pb_ref, d1_ref, d2_ref,
    inv1_ref, diag1_ref, inv2_ref, pinv_ref, diag2_ref,
    f_all, a_all, acc, e_send, e_recv, p_send, p_recv, g_send, g_recv,
    s0_part, s0_in, s0_mid, s0_out, s1_part, s1_in, s1_mid, s1_out,
    fs, fr, a1s, a1r, os, orr, xs, xr, ys, yr, cs, cr, es, er, ps, pr, gs, gr, ss, sr, own_sem,
):
    row, col = lax.axis_index("row"), lax.axis_index("col")
    y, z = row // NZ, row % NZ
    x, yl, core = col // 4, (col // 2) % 2, col % 2

    def remote(src, dst, ss, rs_, to_row, to_col):
        return pltpu.make_async_remote_copy(
            src_ref=src, dst_ref=dst, send_sem=ss, recv_sem=rs_,
            device_id=(to_row, to_col), device_id_type=MESH,
        )

    def z_mate(d):
        return y * NZ + lax.rem(z + d, NZ)

    def y_row(d):
        return lax.rem(y + d, NY) * NZ + z

    def col_of(x_, yl_, core_):
        return x_ * 4 + yl_ * 2 + core_

    y_mate = col_of(x, 1 - yl, core)
    c_mate = col_of(x, yl, 1 - core)
    across = col_of(x + 1 - 2 * lax.rem(x, 2), yl, core)
    outward = col_of(NX - 1 - x, yl, core)

    barrier = pltpu.get_barrier_semaphore()

    for mate in [z_mate(d) for d in range(1, NZ)] + [y_row(d) for d in range(1, NY)]:
        pl.semaphore_signal(barrier, inc=1, device_id=(mate, col), device_id_type=MESH)
    for mate in (across, outward, y_mate, c_mate):
        pl.semaphore_signal(barrier, inc=1, device_id=(row, mate), device_id_type=MESH)
    m0 = p1_ref[0].astype(jnp.float32)
    m1 = p1_ref[1].astype(jnp.float32)
    m2 = p2_ref[0].astype(jnp.float32)
    f_all[0, z] = f1_ref[0] * m0.astype(jnp.bfloat16)
    f_all[1, z] = f1_ref[1] * m1.astype(jnp.bfloat16)
    f_all[2, z] = f2_ref[...] * m2.astype(jnp.bfloat16)
    pl.semaphore_wait(barrier, NZ - 1 + NY - 1 + 4)

    up = y * NZ + lax.rem(z + 1, NZ)
    down = y * NZ + lax.rem(z + NZ - 1, NZ)
    half = B // 2

    def f_copies(stream, step):
        k = min(stream, 2)
        top, bottom = pl.ds(0, half), pl.ds(half, half)
        if stream < 2:
            ups, downs = (pl.ds(0, B), pl.ds(0, B)) if step < 3 else (top, bottom)
        else:
            ups = downs = top if stream == 2 else bottom
        u = f_all.at[k, lax.rem(z + NZ - step, NZ), ups]
        d = f_all.at[k, lax.rem(z + step, NZ), downs]
        copies = []
        if step < 3 or stream != 3:
            copies.append(remote(u, u, fs.at[0, step, stream], fr.at[0, step, stream], up, col))
        if step < 3 or stream != 2:
            copies.append(remote(d, d, fs.at[1, step, stream], fr.at[1, step, stream], down, col))
        return copies

    def f_step(stream, step):
        if step > 0:
            for copy in f_copies(stream, step - 1):
                copy.wait_recv()
        if step < 4:
            for copy in f_copies(stream, step):
                copy.start()

    slot = lax.rem(col, NZ)
    hold = lax.rem(y + x // 2 + 1, 2)
    near = lax.rem(x + 1 + hold, 2)

    def a1_copy(h):
        return remote(
            a_ref.at[h], a_all.at[slot, y], a1s.at[h], a1r.at[y], (2 * h + x // 2) * NZ + z, col
        )

    def own_copy(h):
        return pltpu.make_async_copy(a_ref.at[h], a_all.at[slot, y], own_sem)

    for h in range(2):
        target = 2 * h + x // 2

        @pl.when(target != y)
        def _():
            a1_copy(h).start()

        @pl.when(target == y)
        def _():
            own_copy(h).start()

    def chunk(far, yl_, core_, k):
        s = 1 - near if far else near
        return a_all.at[s * 4 + yl_ * 2 + core_, lax.rem(y + k, NY)]

    def y_copy(k, yl_):
        c = chunk(0, yl_, core, k)
        return remote(c, c, ys.at[k], yr.at[k], row, y_mate)

    def o_copy(other, k):
        c = chunk(0, 1 - yl if other else yl, core, k)
        return remote(c, c, os.at[other, k], orr.at[other, k], row, outward)

    def x_copy(other, k, far=0):
        c = chunk(far, 1 - yl if other else yl, core, k)
        return remote(c, c, xs.at[other, k], xr.at[other, k], row, across)

    def c_copy(far, other, k, core_):
        c = chunk(far, 1 - yl if other else yl, core_, k)
        return remote(c, c, cs.at[far, other, k], cr.at[far, other, k], row, c_mate)

    def near_own(k):
        @pl.when(hold == 1)
        def _():
            if k == 0:
                own_copy(0).wait()
            else:
                other = lax.rem(y + k, NY)
                remote(
                    a_ref.at[0], a_all.at[slot, other], a1s.at[0], a1r.at[other], y_row(1), col
                ).wait_recv()
            y_copy(k, yl).start()
            o_copy(0, k).start()

        @pl.when(hold == 0)
        def _():
            o_copy(0, k).wait_recv()

        x_copy(0, k).start()
        c_copy(0, 0, k, core).start()

    def near_other(k):
        @pl.when(hold == 1)
        def _():
            y_copy(k, 1 - yl).wait_recv()
            o_copy(1, k).start()

        @pl.when(hold == 0)
        def _():
            o_copy(1, k).wait_recv()

        x_copy(1, k).start()
        c_copy(0, 1, k, core).start()

    def far_both(k):
        for other in range(2):
            x_copy(other, k, 1).wait_recv()
            c_copy(1, other, k, core).start()

    def whole(k):
        for far in range(2):
            for other in range(2):
                c_copy(far, other, k, 1 - core).wait_recv()

    y_up = lax.rem(y + 1, NY)
    y_down = lax.rem(y + NY - 1, NY)
    row_up, row_down = y_up * NZ + z, y_down * NZ + z

    def product(y_, k):
        left = jnp.concatenate([a_all[i, y_] for i in range(NZ)], axis=1)
        return mm(left, f_all[k].reshape(NZ * B, B))

    def pair(send, recv, ss, rs_, k):
        return (
            remote(send.at[k, 0], recv.at[k, 0], ss.at[k, 0], rs_.at[k, 0], row_up, col),
            remote(send.at[k, 1], recv.at[k, 1], ss.at[k, 1], rs_.at[k, 1], row_down, col),
        )

    def early(k):
        return pair(e_send, e_recv, es, er, k)

    def plain(k):
        return pair(p_send, p_recv, ps, pr, k)

    def grown(k):
        return pair(g_send, g_recv, gs, gr, k)

    bf, f32 = jnp.bfloat16, jnp.float32

    def send_early(k):
        part = product(lax.rem(y + 2, NY), k).astype(bf)
        e_send[k, 0] = part[:half]
        e_send[k, 1] = part[half:]
        for copy in early(k):
            copy.start()

    def send_up(k):
        part = product(y_up, k)
        acc[0, k] = part[:half]
        p_send[k, 0] = part[half:].astype(bf)
        plain(k)[0].start()

    def send_down(k):
        part = product(y_down, k)
        acc[1, k] = part[half:]
        p_send[k, 1] = part[:half].astype(bf)
        plain(k)[1].start()

    def own(k):
        part = product(y, k)
        acc[2, k] = part[:half]
        acc[3, k] = part[half:]

    def send_grown(k):
        for way in range(2):
            early(k)[way].wait_recv()
            g_send[k, way] = (acc[way, k] + e_recv[k, way].astype(f32)).astype(bf)
            grown(k)[way].start()

    def total(k):
        for way in range(2):
            plain(k)[way].wait_recv()
            grown(k)[way].wait_recv()
        top = acc[2, k] + (g_recv[k, 0].astype(f32) + p_recv[k, 1].astype(f32))
        bottom = acc[3, k] + (p_recv[k, 0].astype(f32) + g_recv[k, 1].astype(f32))
        return jnp.concatenate([top, bottom], axis=0)

    f_step(0, 0)
    f_step(1, 0)
    near_own(0)
    f_step(0, 1)
    f_step(1, 1)
    near_other(0)
    f_step(0, 2)
    near_own(2)
    f_step(1, 2)
    f_step(2, 0)
    far_both(0)
    near_own(1)
    near_other(2)
    f_step(0, 3)
    f_step(3, 0)
    f_step(1, 3)
    f_step(2, 1)
    near_own(3)
    far_both(2)
    near_other(1)
    f_step(3, 1)
    f_step(0, 4)
    f_step(2, 2)
    near_other(3)
    far_both(1)
    whole(2)
    send_early(0)
    f_step(1, 4)
    send_early(1)
    f_step(3, 2)
    f_step(2, 3)
    far_both(3)
    whole(1)
    send_up(0)
    send_up(1)
    whole(3)
    send_down(0)
    send_down(1)
    f_step(3, 3)
    send_grown(0)
    send_grown(1)
    f_step(2, 4)
    f_step(3, 4)
    send_early(2)
    send_up(2)
    send_down(2)
    whole(0)
    own(0)
    own(1)
    own(2)

    def over_z(stage, src, dst):
        return [
            remote(src(d), dst(d), ss.at[stage, d], sr.at[stage, d], z_mate(d), col)
            for d in (4, 3, 5, 2, 6, 1, 7)
        ]

    def over_y(stage, src, dst):
        return [
            remote(src(d), dst(d), ss.at[stage, d], sr.at[stage, d], y_row(d), col) for d in range(1, NY)
        ]

    def z_at(d):
        return lax.rem(z + d, NZ)

    stages = (
        lambda: over_z(0, lambda d: s0_part.at[z_at(d)], lambda d: s0_in.at[d]),
        lambda: over_z(1, lambda d: s1_part.at[z_at(d)], lambda d: s1_in.at[d]),
        lambda: over_y(2, lambda d: s0_mid.at[y], lambda d: s0_mid.at[y]),
        lambda: over_y(3, lambda d: s1_mid.at[y], lambda d: s1_mid.at[y]),
        lambda: over_z(4, lambda d: s0_out.at[z], lambda d: s0_out.at[z]),
        lambda: over_z(5, lambda d: s1_out.at[z], lambda d: s1_out.at[z]),
    )

    def start(stage):
        for copy in stages[stage]():
            copy.start()

    def arrived(stage):
        for copy in stages[stage]():
            copy.wait_recv()

    def sent(stage):
        for copy in stages[stage]():
            copy.wait_send()

    def added(ref):
        return jnp.sum(ref[...].astype(f32), axis=0).astype(bf)

    second = par_ref[0] >= 16
    inv_a = (-total(0) * m0).astype(bf)
    inv_b = (-total(1) * m1).astype(bf)
    parent_cols = jnp.where(second, inv_b, inv_a)
    level_one = jnp.concatenate(
        [mm_t(f_all[0, z], inv_a), mm_t(f_all[1, z], inv_b), mm_t(parent_cols, f_all[2, z])], axis=0
    )
    s0_part[...] = level_one.astype(bf).reshape(NZ, 3 * SLICE, B)
    start(0)
    send_grown(2)
    s0_in[0] = s0_part[z]
    pb = pb_ref[...]
    side = mm(parent_cols, pb)
    inv1_ref[0] = inv_a
    inv1_ref[1] = inv_b
    inv_c = (-(total(2) + side) * m2).astype(bf)
    s1_part[...] = mm_t(f_all[2, z], inv_c).astype(bf).reshape(NZ, SLICE, B)
    start(1)
    s1_in[0] = s1_part[z]
    inv2_ref[...] = inv_c
    arrived(0)
    s0_mid[y] = added(s0_in)
    start(2)
    for stream in range(4):
        for step in range(4):
            for copy in f_copies(stream, step):
                copy.wait_send()
    for k in range(3):
        for copies in (early(k), plain(k), grown(k)):
            for copy in copies:
                copy.wait_send()
    for h in range(2):

        @pl.when(2 * h + x // 2 != y)
        def _():
            a1_copy(h).wait_send()

    @pl.when(hold == 1)
    def _():
        for k in range(NY):
            y_copy(k, yl).wait_send()
            for other in range(2):
                o_copy(other, k).wait_send()

    for k in range(NY):
        for other in range(2):
            x_copy(other, k).wait_send()
            for far in range(2):
                c_copy(far, other, k, core).wait_send()

    arrived(1)
    s1_mid[y] = added(s1_in)
    start(3)
    arrived(2)
    s0_out[z] = added(s0_mid)
    start(4)
    arrived(3)
    s1_out[z] = added(s1_mid)
    start(5)
    for stage in range(4):
        sent(stage)
    arrived(4)
    sums = s0_out[...].reshape(3, B, B).astype(f32)
    diag_a = d1_ref[0] - sums[0]
    diag_b = d1_ref[1] - sums[1]
    diag1_ref[0] = diag_a
    diag1_ref[1] = diag_b
    parent_diag = jnp.where(second, diag_b, diag_a).astype(bf)
    pinv = (-(mm(parent_diag, pb) + sums[2])).astype(bf)
    pinv_ref[...] = pinv
    ahead = d2_ref[...] - mm_t(pb, pinv)
    sent(4)
    arrived(5)
    diag2_ref[...] = ahead - s1_out[...].reshape(B, B).astype(f32)

    sent(5)


def body(anc, one, two, pb, d1, d2, p1, p2, par):
    a = anc.reshape(B, 2, B).transpose(1, 0, 2)
    f1 = one.reshape(B, 2, B).transpose(1, 0, 2)
    vmem = pl.BlockSpec(memory_space=pltpu.VMEM)
    smem = pl.BlockSpec(memory_space=pltpu.SMEM)
    dma = pltpu.SemaphoreType.DMA
    bf, f32 = jnp.bfloat16, jnp.float32
    inv1, diag1, inv2, pinv, diag2 = pl.pallas_call(
        kernel,
        out_shape=(
            jax.ShapeDtypeStruct((2, B, B), bf),
            jax.ShapeDtypeStruct((2, B, B), f32),
            jax.ShapeDtypeStruct((B, B), bf),
            jax.ShapeDtypeStruct((B, B), bf),
            jax.ShapeDtypeStruct((B, B), f32),
        ),
        in_specs=[smem] * 3 + [vmem] * 6,
        out_specs=(vmem,) * 5,
        scratch_shapes=[
            pltpu.VMEM((3, NZ, B, B), bf),
            pltpu.VMEM((NZ, NY, B, B), bf),
            pltpu.VMEM((4, 3, B // 2, B), f32),
        ]
        + [pltpu.VMEM((3, 2, B // 2, B), bf)] * 6
        + [
            pltpu.VMEM((NZ, 3 * SLICE, B), bf), pltpu.VMEM((NZ, 3 * SLICE, B), bf),
            pltpu.VMEM((NY, 3 * SLICE, B), bf), pltpu.VMEM((NZ, 3 * SLICE, B), bf),
            pltpu.VMEM((NZ, SLICE, B), bf), pltpu.VMEM((NZ, SLICE, B), bf),
            pltpu.VMEM((NY, SLICE, B), bf), pltpu.VMEM((NZ, SLICE, B), bf),
        ]
        + [
            dma((2, 4, 4)), dma((2, 4, 4)),
            dma((2,)), dma((NY,)),
            dma((2, NY)), dma((2, NY)),
            dma((2, NY)), dma((2, NY)),
            dma((NY,)), dma((NY,)),
            dma((2, 2, NY)), dma((2, 2, NY)),
            dma((3, 2)), dma((3, 2)),
            dma((3, 2)), dma((3, 2)),
            dma((3, 2)), dma((3, 2)),
            dma((6, NZ)), dma((6, NZ)),
            dma(()),
        ],
        compiler_params=pltpu.CompilerParams(
            collective_id=0, has_side_effects=True, vmem_limit_bytes=40 * 1024 * 1024
        ),
    )(
        p1.reshape(2), p2.reshape(1), par.reshape(1), a, f1, two.reshape(B, B),
        pb.reshape(B, B), d1.reshape(2, B, B), d2.reshape(B, B),
    )
    return (
        inv1.transpose(1, 0, 2).reshape(one.shape),
        diag1.reshape(d1.shape),
        inv2.reshape(two.shape),
        pinv.reshape(pb.shape),
        diag2.reshape(d2.shape),
    )


def solution(mesh):
    placed = (
        P(None, "row", None, None, "col", None),
        P(None, "row", None, None, "col", None),
        P(None, "row", None, None, "col", None),
        P(None, "col", None, None),
        P(None, "col", None, None),
        P(None, "col", None, None),
        P(None, "row", None, "col"),
        P(None, "row", None, "col"),
        P(None, "col"),
    )
    return jax.shard_map(
        body,
        mesh=mesh,
        in_specs=placed,
        out_specs=(
            P(None, "row", None, None, "col", None),
            P(None, "col", None, None),
            P(None, "row", None, None, "col", None),
            P(None, "col", None, None),
            P(None, "col", None, None),
        ),
        check_vma=False,
    )
```
